32 devices in a mesh: grid: 8 (over z, y), vis: 4 (over x, core).
Axes of the slice: x: 2, y: 2, z: 4, core: 2. Of those that a mesh axis runs over, the one named last changes fastest.
Arguments:
- vis_coords: float32 [8, 256, 2, 512], P('grid', 'vis'), may hold values from 0 to 64
- vis_values: float32 [8, 256, 2, 512], P('grid', 'vis'), may hold values from -6 to 6
- tile_index: int32 [8, 256], P('grid', 'vis'), may hold values from 0 to 63
Outputs:
- facets: float32 [8, 2, 1024, 1024], P('grid', None, 'vis')
The draws below stay inside these ranges and needn't reach their ends.
Inputs may be any that keep to these rules, and one draw needn't show every extreme that they name: `tile_index`: tile a * 8 + e covers subgrid rows from a * 64 and columns from e * 64.
All inputs are finite; a program needn't handle non-finite values.
Results may differ from the reference program's by a relative error of at most 0.014.
Values may be sent and summed in bfloat16 or wider, within the bound.
A program may use at most 64 MiB of HBM per device.

```python
import math
import jax
import jax.numpy as jnp
from jax import lax

SUB = 512
FAC = 1024
CONTRIB = 64
TILE = 64
BLK = 512
BLK_DEV = 64
NBLK = 8
VBLOCKS = 256
SUBGRIDS = 8
N_GRID = 8
N_VIS = 4


def touch_ends(entries, stream_key, least, high):
    shape = entries.shape
    index_at = [jax.random.randint(jax.random.fold_in(stream_key, axis), (), 0, shape[axis]) for axis in range(len(shape))]
    entries = entries.at[tuple(index_at)].set(least)
    longest = shape.index(max(shape))
    index_at[longest] = (index_at[longest] + 1) % shape[longest]
    return entries.at[tuple(index_at)].set(high)


def block_scale(stream_key, shape, split, smallest, largest):
    loudness, own = 1.0, jax.random.fold_in(stream_key, 6)
    for position, shards_of in split:
        heights = jnp.exp(jax.random.uniform(jax.random.fold_in(own, position), (shards_of,), jnp.float32, smallest / len(split), largest / len(split)))
        loudness = loudness * jnp.repeat(heights, shape[position] // shards_of).reshape([-1 if axis == position else 1 for axis in range(len(shape))])
    return loudness


def noise(key, dims, width, reach, pieces=(), kind=jnp.bfloat16):
    result = jax.random.normal(key, dims, jnp.float32) * width
    if len(pieces) > 0:
        result = block_scale(key, dims, pieces, -0.22, 0.18) * result
    return jnp.clip(result, min=-reach, max=reach).astype(kind)


def setup_inputs(seed: int = 0) -> dict:
    seeds = jax.random.split(jax.random.key(seed), 4)
    vis_coords = jnp.clip(64.0 * jax.random.uniform(seeds[0], (SUBGRIDS, VBLOCKS, 2, BLK), jnp.float32) ** block_scale(seeds[0], (SUBGRIDS, VBLOCKS, 2, BLK), ((0, 8), (1, 4)), -0.2, 0.2), 0.0, 64.0)
    vis_values = noise(seeds[1], (SUBGRIDS, VBLOCKS, 2, BLK), 1.0, 6.0, ((0, 8), (1, 4)), jnp.float32)
    tile_index = touch_ends(jax.random.randint(seeds[2], (SUBGRIDS, VBLOCKS), 0, (SUB // TILE) * (SUB // TILE)), jax.random.fold_in(seeds[2], 1), 0, ((SUB // TILE) * (SUB // TILE)) - 1).astype(jnp.int32)
    return dict(vis_coords=vis_coords, vis_values=vis_values, tile_index=tile_index)


taper_scale = 16.0

def phase_pair(frequencies, points, length):
    phases = frequencies[:, None] * points[None, :] % length
    angles = phases.astype(jnp.float32) * (2.0 * math.pi / length)
    return (jnp.cos(angles), jnp.sin(angles))

def kernel_rows(places):
    pixels = jnp.arange(TILE, dtype=jnp.float32)
    distance = pixels - places[..., None]
    scaled = distance / taper_scale
    return jnp.sinc(distance) * jnp.exp(-scaled * scaled)

def exact_dot(first, second):
    return jnp.dot(first.astype(jnp.float32), second.astype(jnp.float32), precision=lax.Precision.HIGHEST, preferred_element_type=jnp.float32)

def grid_blocks(coords, values, tile_ids):
    across = SUB // TILE
    weights_u = kernel_rows(coords[:, 0])
    weights_v = kernel_rows(coords[:, 1])
    weighted = weights_u[:, None] * values[:, :, :, None]
    patches = jnp.einsum('bcnx,bny->bcxy', weighted, weights_v, precision=lax.Precision.HIGHEST, preferred_element_type=jnp.float32)
    onehot = (tile_ids[None, :] == jnp.arange(across * across, dtype=jnp.int32)[:, None]).astype(jnp.float32)
    placed = jnp.dot(onehot, patches.reshape(coords.shape[0], 2 * TILE * TILE), precision=lax.Precision.HIGHEST, preferred_element_type=jnp.float32)
    return placed.reshape(across, across, 2, TILE, TILE).transpose(0, 3, 2, 1, 4).reshape(SUB, 2, SUB)

def complex_block(part_real, part_imag):
    return jnp.concatenate([jnp.concatenate([part_real, part_imag], 1), jnp.concatenate([-part_imag, part_real], 1)], 0)

def reference(vis_coords, vis_values, tile_index):
    groups = N_GRID // NBLK
    column_count = groups * CONTRIB
    unitary = 1.0 / math.sqrt(SUB)
    spectrum = jnp.arange(SUB, dtype=jnp.int32)
    tab_real, tab_imag = phase_pair(spectrum, jnp.arange(column_count, dtype=jnp.int32), SUB)
    col_table = jnp.concatenate([jnp.concatenate([tab_real, -tab_imag], 1), jnp.concatenate([tab_imag, tab_real], 1)], 0).astype(jnp.bfloat16)
    rows_real, rows_imag = phase_pair(spectrum, spectrum, SUB)
    left_side = jnp.concatenate([rows_real, -rows_imag], 1).astype(jnp.bfloat16)

    def one_subgrid(inputs):
        coords, values, tile_ids = inputs
        running = jnp.zeros((SUB, 2, SUB), jnp.float32)
        for member in range(N_VIS):
            first = member * BLK_DEV
            placed = grid_blocks(coords[first:first + BLK_DEV], values[first:first + BLK_DEV], tile_ids[first:first + BLK_DEV])
            running = running + lax.optimization_barrier(placed.astype(jnp.bfloat16)).astype(jnp.float32)
        summed = running.astype(jnp.bfloat16)
        images = (exact_dot(summed.reshape(SUB, 2 * SUB), col_table) * unitary).astype(jnp.bfloat16).reshape(SUB, 2, column_count)
        stacked = complex_block(images[:, 0], images[:, 1])
        spectra = (exact_dot(left_side, stacked) * unitary).astype(jnp.bfloat16)
        return spectra.reshape(NBLK, CONTRIB, 2, groups, CONTRIB).transpose(3, 0, 2, 1, 4).reshape(N_GRID, 2, CONTRIB, CONTRIB)
    contribs = lax.map(one_subgrid, (vis_coords, vis_values, tile_index))
    embed_real, embed_imag = phase_pair(jnp.arange(FAC, dtype=jnp.int32), spectrum, FAC)
    embed_left = jnp.concatenate([embed_real, embed_imag], 1).astype(jnp.bfloat16)
    out_real, out_imag = phase_pair(jnp.arange(column_count, dtype=jnp.int32), jnp.arange(FAC, dtype=jnp.int32), FAC)
    real_right = jnp.concatenate([out_real, -out_imag], 0).astype(jnp.bfloat16)
    imag_right = jnp.concatenate([out_imag, out_real], 0).astype(jnp.bfloat16)
    sines = jnp.sin(math.pi * (jnp.arange(FAC, dtype=jnp.float32) + 0.5) / FAC)
    taper_rows = 0.25 + 0.75 * sines * sines
    weight = taper_rows[:, None] * taper_rows[None, :] * (1.0 / math.sqrt(CONTRIB * groups))

    def one_facet(facet_id):
        received = lax.dynamic_index_in_dim(contribs, facet_id, 1, keepdims=False)
        blocks = received.reshape(groups, NBLK, 2, CONTRIB, CONTRIB).transpose(1, 3, 2, 0, 4)
        part_real = blocks[:, :, 0].reshape(SUB, column_count)
        part_imag = blocks[:, :, 1].reshape(SUB, column_count)
        mixture = (exact_dot(embed_left, complex_block(part_real, part_imag)) * unitary).astype(jnp.bfloat16)
        return jnp.stack([exact_dot(mixture, real_right) * weight, exact_dot(mixture, imag_right) * weight])
    return lax.map(one_facet, jnp.arange(N_GRID, dtype=jnp.int32))
```

```python
import functools
import math

import jax
import jax.numpy as jnp
import ml_dtypes
import numpy as np
from jax import lax
from jax.experimental import pallas as pl
from jax.experimental.pallas import tpu as pltpu
from jax.sharding import PartitionSpec as P

SUB = 512
FAC = 1024
CONTRIB = 64
TILE = 64
NBLK = 8
LANES = 2 * CONTRIB
TAPER_SCALE = 16.0
SAVES = 4
JOINT = 16
ROOM = 32 * 2**20
MESH = pl.DeviceIdType.MESH


def phase_pair(frequencies, points, length):
    phases = (frequencies[:, None] * points[None, :]) % length
    angles = phases * (2.0 * math.pi / length)
    return np.cos(angles).astype(np.float32), np.sin(angles).astype(np.float32)


def as_bf16(array):
    return array.astype(ml_dtypes.bfloat16)


def column_table(groups):
    cos, sin = phase_pair(np.arange(SUB), np.arange(groups * CONTRIB), SUB)
    across = SUB // TILE
    table = np.zeros((across, 2, TILE, groups, 4, CONTRIB), np.float32)
    cos = cos.reshape(across, TILE, groups, CONTRIB)
    sin = sin.reshape(across, TILE, groups, CONTRIB)
    table[:, 0, :, :, 0], table[:, 1, :, :, 0] = cos, sin
    table[:, 0, :, :, 1], table[:, 1, :, :, 1] = -sin, cos
    table[:, :, :, :, 2] = -table[:, :, :, :, 1]
    table[:, :, :, :, 3] = table[:, :, :, :, 0]
    return as_bf16(table.reshape(2 * SUB, groups * 4 * CONTRIB))


def row_table(vis_count):
    quarter = CONTRIB // vis_count
    order = np.arange(SUB).reshape(NBLK, vis_count, quarter).transpose(1, 0, 2).reshape(SUB)
    cos, sin = phase_pair(order, np.arange(SUB), SUB)
    return as_bf16(np.concatenate([cos, -sin], 1))


def embed_table(vis_count):
    order = np.arange(SUB).reshape(NBLK, vis_count, CONTRIB // vis_count).transpose(1, 0, 2)
    cos, sin = phase_pair(np.arange(FAC), order.reshape(SUB), FAC)
    return as_bf16(np.concatenate([cos, sin], 1))


def output_table(groups):
    cos, sin = phase_pair(np.arange(groups * CONTRIB), np.arange(FAC), FAC)
    cos = cos.reshape(groups, CONTRIB, FAC)
    sin = sin.reshape(groups, CONTRIB, FAC)
    real = np.stack([cos, -sin], 1).reshape(groups * LANES, FAC)
    imag = np.stack([sin, cos], 1).reshape(groups * LANES, FAC)
    return as_bf16(np.concatenate([real, imag], 1))


def taper():
    sines = np.sin(np.pi * (np.arange(FAC) + 0.5) / FAC)
    return 0.25 + 0.75 * sines * sines


SINE = [(-1.0) ** k * math.pi ** (2 * k) / math.factorial(2 * k + 1) for k in range(7)]


GAUSS = math.log2(math.e) / (TAPER_SCALE * TAPER_SCALE)
MIDDLE = TILE // 2


def swapped(index, bits):
    result = index
    bit = 1
    while bit <= bits:
        if bits & bit:
            result = result + bit * (1 - 2 * ((index // bit) % 2))
        bit *= 2
    return result


def chains(tile_row, chain):
    blocks = tile_row.shape[1]
    across = jnp.broadcast_to(tile_row[...], (blocks, blocks))
    down = across.T
    above = lax.broadcasted_iota(jnp.int32, (blocks, blocks), 0)
    beside = lax.broadcasted_iota(jnp.int32, (blocks, blocks), 1)
    before = jnp.where((across == down) & (above < beside), above + 1, 0)
    latest = jnp.where(down == beside, above + 1, 0)
    for k, table in enumerate((before, latest)):
        while table.shape[0] > 8:
            half = table.shape[0] // 2
            table = jnp.maximum(table[:half], table[half:])
        for turn in (4, 2, 1):
            table = jnp.maximum(table, pltpu.roll(table, turn, 0))
        chain[k : k + 1, :blocks] = table[:1]


def subgrid_kernel(
    grid_count, vis_count, unitary,
    tiles_hbm, coords_hbm, values_hbm, col_hbm, row_hbm, embed_hbm, scale_hbm, out,
    tile_row, chain, links, coords, values, levels, spread, sums,
    col, table, embed, scale, part, spectra, pieces, gathered,
    tile_sem, link_sem, visible_sem, load_sem, send1, recv1, send2, recv2,
):
    me_g, me_v = lax.axis_index("grid"), lax.axis_index("vis")
    groups = grid_count // NBLK
    rows_here = out.shape[0]
    quarter = CONTRIB // vis_count
    count = grid_count * vis_count
    mine = pl.ds(pl.multiple_of(me_v * rows_here, rows_here), rows_here)
    blocks, axes, visible = coords.shape
    f32, bf16 = jnp.float32, jnp.bfloat16
    steps = blocks // JOINT

    def loads(i):
        part = pl.ds(i * JOINT, JOINT)
        return (
            pltpu.make_async_copy(coords_hbm.at[part], coords.at[part], visible_sem.at[i, 0]),
            pltpu.make_async_copy(values_hbm.at[part], values.at[part], visible_sem.at[i, 1]),
        )

    tile_load = pltpu.make_async_copy(tiles_hbm, tile_row, tile_sem)
    tile_load.start()
    for i in range(steps):
        for load in loads(i):
            load.start()
    peers = [
        (swapped(me_g, g), swapped(me_v, v))
        for g in range(grid_count - 1, -1, -1)
        for v in range(vis_count - 1, -1, -1)
        if g or v
    ]
    barrier = pltpu.get_barrier_semaphore()
    for peer in peers:
        pl.semaphore_signal(barrier, inc=1, device_id=peer, device_id_type=MESH)
    tables = [
        pltpu.make_async_copy(col_hbm, col, load_sem.at[0]),
        pltpu.make_async_copy(row_hbm, table, load_sem.at[1]),
        pltpu.make_async_copy(embed_hbm.at[mine], embed, load_sem.at[2]),
        pltpu.make_async_copy(scale_hbm.at[mine], scale, load_sem.at[3]),
    ]
    for load in tables:
        load.start()
    sums[0] = jnp.zeros((TILE, 2 * TILE), f32)
    tile_load.wait()
    chains(tile_row, chain)
    link_load = pltpu.make_async_copy(chain, links, link_sem)
    link_load.start()
    row = lax.broadcasted_iota(jnp.int32, (16, 1), 0).astype(f32)
    lean = (row[:8] - MIDDLE) * (2.0 * GAUSS)
    spots = [
        jnp.broadcast_to((row + 16.0 * a).astype(bf16), (16, visible)) for a in range(TILE // 16)
    ]
    even = lax.broadcasted_iota(jnp.int32, (2 * JOINT, visible), 0) % 2 == 0

    def prepare(b):
        part = pl.ds(b * JOINT, JOINT)
        where = coords[part].reshape(JOINT * axes, visible)
        nearest = jnp.floor(where + 0.5)
        offset = where - nearest
        offset = jnp.where(jnp.abs(offset) < 1e-10, 1e-10, offset)
        square = offset * offset
        wave = square * SINE[5] + SINE[4]
        for k in range(3, -1, -1):
            wave = wave * square + SINE[k]
        half = nearest * 0.5
        odd = (half - jnp.floor(half)) * 4.0 - 1.0
        centred = where - MIDDLE
        wave = (wave * offset) * (odd * jnp.exp2(centred * centred * -GAUSS))
        rows = 2 * JOINT
        wave = wave * jnp.where(even, pltpu.roll(wave, rows - 1, 0), pltpu.roll(wave, 1, 0))
        spread[0] = centred
        spread[1] = nearest
        spread[2] = offset
        growth = jnp.exp2(centred * (16.0 * GAUSS))
        spread[3] = growth
        growth = growth * growth
        spread[4] = growth
        spread[5] = growth * growth
        levels[...] = values[part].reshape(rows, visible) * wave

    def wide(ref, i):
        return jnp.broadcast_to(ref[i : i + 1], (16, visible))

    def rows(ref, i, paired):
        near = wide(ref.at[1], i).astype(bf16)
        apart = wide(ref.at[2], i).astype(bf16)
        low = jnp.exp2(jnp.broadcast_to(ref[0, i : i + 1], (8, visible)) * lean)
        high = low * jnp.broadcast_to(ref[3, i : i + 1], (8, visible))
        rise = jnp.concatenate([low, high], 0).astype(bf16)
        growth = wide(ref.at[4], i).astype(bf16)
        result = []
        if not paired:
            for a in range(TILE // 16):
                result.append(rise * pl.reciprocal((spots[a] - near) - apart, approx=True))
                rise = rise * growth
            return result
        twice = wide(ref.at[5], i).astype(bf16)
        for a in range(0, TILE // 16, 2):
            here = (spots[a] - near) - apart
            next = (spots[a + 1] - near) - apart
            ratio = rise * pl.reciprocal(here * next, approx=True)
            result += [ratio * next, (ratio * growth) * here]
            rise = rise * twice
        return result

    def several(b, carry):
        for load in loads(b):
            load.wait()
        prepare(b)
        for i in range(JOINT):
            along = jnp.concatenate(rows(spread, 2 * i, True), 0)
            down = rows(spread, 2 * i + 1, False)
            right = []
            for c in range(2):
                level = wide(levels, 2 * i + c).astype(bf16)
                right += [d * level for d in down]
            patch = lax.dot_general(
                along, jnp.concatenate(right, 0), (((1,), (1,)), ((), ())), preferred_element_type=f32
            )
            k = b * JOINT + i
            sums[k + 1] = sums[links[0, k]] + patch
        return carry

    link_load.wait()
    lax.fori_loop(0, steps, several, 0)

    down = lax.broadcasted_iota(jnp.int32, (TILE, 2 * TILE), 0) - MIDDLE
    along = lax.broadcasted_iota(jnp.int32, (TILE, 2 * TILE), 1) % TILE - MIDDLE
    power = (down * down + along * along).astype(jnp.float32)
    flip = 1.0 - 2.0 * ((down + along + 2 * TILE) % 2).astype(jnp.float32)
    fall = flip * jnp.exp2(power * -GAUSS)
    for a in range(SUB // TILE):
        for e in range(SUB // TILE):
            spot = (slice(a * TILE, (a + 1) * TILE), slice(e * 2 * TILE, (e + 1) * 2 * TILE))
            part[spot] = (sums[links[1, a * (SUB // TILE) + e]] * fall).astype(bf16)
    for load in tables:
        load.wait()
    for g in range(groups):
        image = jnp.dot(
            part[...], col[:, 2 * LANES * g : 2 * LANES * (g + 1)], preferred_element_type=jnp.float32
        )
        image = (image * unitary).astype(jnp.bfloat16)
        both = jnp.concatenate([image[:, :LANES], image[:, LANES:]], 0)
        result = jnp.dot(table[...], both, preferred_element_type=jnp.float32)
        result = (result * unitary).astype(jnp.bfloat16)
        spectra[:, NBLK * g : NBLK * (g + 1)] = result.reshape(vis_count, NBLK, quarter, LANES)

    pl.semaphore_wait(barrier, count - 1)

    def scatter(peer):
        return pltpu.make_async_remote_copy(
            src_ref=spectra.at[peer[1], peer[0]], dst_ref=pieces.at[me_g * vis_count + me_v],
            send_sem=send1, recv_sem=recv1, device_id=peer, device_id_type=MESH,
        )

    def gather(j):
        spot = gathered.at[me_v]
        return pltpu.make_async_remote_copy(
            src_ref=spot, dst_ref=spot, send_sem=send2.at[j], recv_sem=recv2.at[j],
            device_id=(me_g, swapped(me_v, j)), device_id_type=MESH,
        )

    for peer in peers:
        scatter(peer).start()
    pieces[me_g * vis_count + me_v] = spectra[me_v, me_g]
    others = pieces.at[pl.ds(0, count - 1)]
    pltpu.make_async_copy(others, others, recv1).wait()
    whole = pieces[...].reshape(grid_count, vis_count, quarter, LANES).astype(f32)
    gathered[me_v] = jnp.sum(whole, 1).astype(jnp.bfloat16)
    for j in range(vis_count - 1, 0, -1):
        gather(j).start()
    for j in range(vis_count - 1, 0, -1):
        gather(j).wait_recv()
    sign = jnp.where(lax.broadcasted_iota(jnp.int32, (1, LANES), 1) < CONTRIB, -1.0, 1.0)
    for g in range(groups):
        straight = gathered[:, NBLK * g : NBLK * (g + 1)].reshape(SUB, LANES)
        turned = pltpu.roll(straight.astype(f32), CONTRIB, 1) * sign
        both = jnp.concatenate([straight, turned.astype(jnp.bfloat16)], 0)
        mixture = jnp.dot(embed[...], both, preferred_element_type=jnp.float32)
        out[:, LANES * g : LANES * (g + 1)] = (mixture * scale[...]).astype(jnp.bfloat16)
    pltpu.make_async_copy(others, others, send1).wait()
    for j in range(1, vis_count):
        gather(j).wait_send()


def image_kernel(mixture, table, weight, out, image, save_sem):
    rows_here = mixture.shape[0]
    saves = []
    for c in range(2):
        for h in range(SAVES):
            part = slice(h * (rows_here // SAVES), (h + 1) * (rows_here // SAVES))
            result = jnp.dot(
                mixture[part], table[:, c * FAC : (c + 1) * FAC], preferred_element_type=jnp.float32
            )
            image[c, part] = result * weight[...]
            saves.append(
                pltpu.make_async_copy(
                    image.at[c, part], out.at[0, c, part], save_sem.at[c * SAVES + h]
                )
            )
            saves[-1].start()
    for save in saves:
        save.wait()


def shards(grid_count, vis_count, vis_coords, vis_values, tile_index):
    groups = grid_count // NBLK
    quarter = CONTRIB // vis_count
    rows_here = FAC // vis_count
    unitary = 1.0 / math.sqrt(SUB)
    bf16, f32 = jnp.bfloat16, jnp.float32
    far = pl.BlockSpec(memory_space=pltpu.HBM)
    inside = pl.BlockSpec(memory_space=pltpu.VMEM)
    dma = pltpu.SemaphoreType.DMA
    blocks = vis_coords.shape[1]
    visible = vis_coords.shape[3]
    row_scale = taper() * (unitary / math.sqrt(CONTRIB * groups))
    row_scale = np.broadcast_to(row_scale[:, None], (FAC, LANES)).astype(np.float32)
    mixture = pl.pallas_call(
        functools.partial(subgrid_kernel, grid_count, vis_count, unitary),
        out_shape=jax.ShapeDtypeStruct((rows_here, groups * LANES), bf16),
        in_specs=[far] * 7,
        out_specs=inside,
        scratch_shapes=[
            pltpu.VMEM((1, blocks), jnp.int32),
            pltpu.VMEM((2, LANES), jnp.int32),
            pltpu.SMEM((2, LANES), jnp.int32),
            pltpu.VMEM((blocks, 2, visible), f32),
            pltpu.VMEM((blocks, 2, visible), f32),
            pltpu.VMEM((2 * JOINT, visible), f32),
            pltpu.VMEM((6, 2 * JOINT, visible), f32),
            pltpu.VMEM((blocks + 1, TILE, 2 * TILE), f32),
            pltpu.VMEM((2 * SUB, 2 * LANES * groups), bf16),
            pltpu.VMEM((SUB, 2 * SUB), bf16),
            pltpu.VMEM((rows_here, 2 * SUB), bf16),
            pltpu.VMEM((rows_here, LANES), f32),
            pltpu.VMEM((SUB, 2 * SUB), bf16),
            pltpu.VMEM((vis_count, grid_count, quarter, LANES), bf16),
            pltpu.VMEM((grid_count * vis_count, quarter, LANES), bf16),
            pltpu.VMEM((vis_count, grid_count, quarter, LANES), bf16),
            dma,
            dma,
            dma((blocks // JOINT, 2)),
            dma((4,)),
            dma,
            dma,
            dma((vis_count,)),
            dma((vis_count,)),
        ],
        compiler_params=pltpu.CompilerParams(
            collective_id=0, has_side_effects=True, vmem_limit_bytes=ROOM
        ),
        cost_estimate=pl.CostEstimate(flops=10**10, bytes_accessed=10**6, transcendentals=10**6),
        name="subgrids",
    )(
        *[
            pltpu.with_memory_space_constraint(array, pltpu.HBM)
            for array in (
                tile_index,
                vis_coords.reshape(blocks, 2, visible),
                vis_values.reshape(blocks, 2, visible),
                jnp.asarray(column_table(groups)),
                jnp.asarray(row_table(vis_count)),
                jnp.asarray(embed_table(vis_count)),
                jnp.asarray(row_scale),
            )
        ]
    )

    return pl.pallas_call(
        image_kernel,
        out_shape=jax.ShapeDtypeStruct((1, 2, rows_here, FAC), f32),
        in_specs=[inside] * 3,
        out_specs=far,
        scratch_shapes=[pltpu.VMEM((2, rows_here, FAC), f32), dma((2 * SAVES,))],
        compiler_params=pltpu.CompilerParams(vmem_limit_bytes=ROOM),
        name="images",
    )(
        mixture,
        jnp.asarray(output_table(groups)),
        jnp.asarray(taper()[None, :].astype(np.float32)),
    )


def solution(mesh):
    placed = (P("grid", "vis", None, None), P("grid", "vis", None, None), P("grid", "vis"))
    body = functools.partial(shards, mesh.shape["grid"], mesh.shape["vis"])
    return jax.shard_map(
        body, mesh=mesh, in_specs=placed, out_specs=P("grid", None, "vis", None), check_vma=False
    )
```

```python
import functools
import math

import jax
import jax.numpy as jnp
import ml_dtypes
import numpy as np
from jax import lax
from jax.experimental import pallas as pl
from jax.experimental.pallas import tpu as pltpu
from jax.sharding import PartitionSpec as P

SUB = 512
FAC = 1024
CONTRIB = 64
TILE = 64
NBLK = 8
LANES = 2 * CONTRIB
TAPER_SCALE = 16.0
SAVES = 4
JOINT = 16
ROOM = 32 * 2**20
MESH = pl.DeviceIdType.MESH


def phase_pair(frequencies, points, length):
    phases = (frequencies[:, None] * points[None, :]) % length
    angles = phases * (2.0 * math.pi / length)
    return np.cos(angles).astype(np.float32), np.sin(angles).astype(np.float32)


def as_bf16(array):
    return array.astype(ml_dtypes.bfloat16)


def column_table(groups):
    cos, sin = phase_pair(np.arange(SUB), np.arange(groups * CONTRIB), SUB)
    across = SUB // TILE
    table = np.zeros((across, 2, TILE, groups, 4, CONTRIB), np.float32)
    cos = cos.reshape(across, TILE, groups, CONTRIB)
    sin = sin.reshape(across, TILE, groups, CONTRIB)
    table[:, 0, :, :, 0], table[:, 1, :, :, 0] = cos, sin
    table[:, 0, :, :, 1], table[:, 1, :, :, 1] = -sin, cos
    table[:, :, :, :, 2] = -table[:, :, :, :, 1]
    table[:, :, :, :, 3] = table[:, :, :, :, 0]
    return as_bf16(table.reshape(2 * SUB, groups * 4 * CONTRIB))


def row_table():
    order = np.arange(SUB).reshape(NBLK, 2, CONTRIB // 2).transpose(1, 0, 2).reshape(SUB)
    cos, sin = phase_pair(order, np.arange(SUB), SUB)
    return as_bf16(np.concatenate([cos, -sin], 1))


def embed_table():
    order = np.arange(SUB).reshape(NBLK, 2, CONTRIB // 2).transpose(1, 0, 2).reshape(2, -1)
    parts = [np.concatenate(phase_pair(np.arange(FAC), spots, FAC), 1) for spots in order]
    return as_bf16(np.stack(parts))


def output_table(groups):
    cos, sin = phase_pair(np.arange(groups * CONTRIB), np.arange(FAC), FAC)
    cos = cos.reshape(groups, CONTRIB, FAC)
    sin = sin.reshape(groups, CONTRIB, FAC)
    real = np.stack([cos, -sin], 1).reshape(groups * LANES, FAC)
    imag = np.stack([sin, cos], 1).reshape(groups * LANES, FAC)
    return as_bf16(np.concatenate([real, imag], 1))


def taper():
    sines = np.sin(np.pi * (np.arange(FAC) + 0.5) / FAC)
    return 0.25 + 0.75 * sines * sines


SINE = [(-1.0) ** k * math.pi ** (2 * k) / math.factorial(2 * k + 1) for k in range(7)]


GAUSS = math.log2(math.e) / (TAPER_SCALE * TAPER_SCALE)
MIDDLE = TILE // 2


def swapped(index, bits):
    result = index
    bit = 1
    while bit <= bits:
        if bits & bit:
            result = result + bit * (1 - 2 * ((index // bit) % 2))
        bit *= 2
    return result


def chains(tile_row, chain):
    blocks = tile_row.shape[1]
    across = jnp.broadcast_to(tile_row[...], (blocks, blocks))
    down = across.T
    above = lax.broadcasted_iota(jnp.int32, (blocks, blocks), 0)
    beside = lax.broadcasted_iota(jnp.int32, (blocks, blocks), 1)
    before = jnp.where((across == down) & (above < beside), above + 1, 0)
    latest = jnp.where(down == beside, above + 1, 0)
    for k, table in enumerate((before, latest)):
        while table.shape[0] > 8:
            half = table.shape[0] // 2
            table = jnp.maximum(table[:half], table[half:])
        for turn in (4, 2, 1):
            table = jnp.maximum(table, pltpu.roll(table, turn, 0))
        chain[k : k + 1, :blocks] = table[:1]


def subgrid_kernel(
    grid_count, vis_count, unitary,
    tiles_hbm, coords_hbm, values_hbm, col_hbm, row_hbm, embed_hbm, scale_hbm, out,
    tile_row, chain, links, coords, values, levels, spread, sums,
    col, table, embed, scale, part, lent, borrowed, spectra, pieces, gathered,
    tile_sem, link_sem, visible_sem, load_sem, share_sem, gather_sem, send1, recv1,
):
    me_g, me_v = lax.axis_index("grid"), lax.axis_index("vis")
    groups = grid_count // NBLK
    rows_here = out.shape[0]
    half = CONTRIB // 2
    mine = pl.ds(pl.multiple_of(me_v * rows_here, rows_here), rows_here)
    blocks, axes, visible = coords.shape
    f32, bf16 = jnp.float32, jnp.bfloat16
    steps = blocks // JOINT

    def loads(i):
        part = pl.ds(i * JOINT, JOINT)
        return (
            pltpu.make_async_copy(coords_hbm.at[part], coords.at[part], visible_sem.at[i, 0]),
            pltpu.make_async_copy(values_hbm.at[part], values.at[part], visible_sem.at[i, 1]),
        )

    tile_load = pltpu.make_async_copy(tiles_hbm, tile_row, tile_sem)
    tile_load.start()
    for i in range(steps):
        for load in loads(i):
            load.start()
    pairs = vis_count // 2
    core, side = me_v % 2, me_v // 2
    mate = (me_g, swapped(me_v, 1))
    peers = [
        (swapped(me_g, g), swapped(me_v, 2 * x))
        for g in range(grid_count - 1, -1, -1)
        for x in range(pairs - 1, -1, -1)
        if g or x
    ]
    barrier = pltpu.get_barrier_semaphore()
    greeted = peers + [mate]
    for peer in greeted:
        pl.semaphore_signal(barrier, inc=1, device_id=peer, device_id_type=MESH)
    tables = [
        pltpu.make_async_copy(col_hbm, col, load_sem.at[0]),
        pltpu.make_async_copy(row_hbm, table, load_sem.at[1]),
        pltpu.make_async_copy(embed_hbm.at[core, mine], embed.at[0], load_sem.at[2]),
        pltpu.make_async_copy(embed_hbm.at[1 - core, mine], embed.at[1], load_sem.at[3]),
        pltpu.make_async_copy(scale_hbm.at[mine], scale, load_sem.at[4]),
    ]
    for load in tables:
        load.start()
    sums[0] = jnp.zeros((TILE, 2 * TILE), f32)
    tile_load.wait()
    chains(tile_row, chain)
    link_load = pltpu.make_async_copy(chain, links, link_sem)
    link_load.start()
    row = lax.broadcasted_iota(jnp.int32, (16, 1), 0).astype(f32)
    lean = (row[:8] - MIDDLE) * (2.0 * GAUSS)
    spots = [
        jnp.broadcast_to((row + 16.0 * a).astype(bf16), (16, visible)) for a in range(TILE // 16)
    ]
    even = lax.broadcasted_iota(jnp.int32, (2 * JOINT, visible), 0) % 2 == 0

    def prepare(b):
        part = pl.ds(b * JOINT, JOINT)
        where = coords[part].reshape(JOINT * axes, visible)
        nearest = jnp.floor(where + 0.5)
        offset = where - nearest
        offset = jnp.where(jnp.abs(offset) < 1e-10, 1e-10, offset)
        square = offset * offset
        wave = square * SINE[5] + SINE[4]
        for k in range(3, -1, -1):
            wave = wave * square + SINE[k]
        half = nearest * 0.5
        odd = (half - jnp.floor(half)) * 4.0 - 1.0
        centred = where - MIDDLE
        wave = (wave * offset) * (odd * jnp.exp2(centred * centred * -GAUSS))
        rows = 2 * JOINT
        wave = wave * jnp.where(even, pltpu.roll(wave, rows - 1, 0), pltpu.roll(wave, 1, 0))
        spread[0] = centred
        spread[1] = nearest
        spread[2] = offset
        growth = jnp.exp2(centred * (16.0 * GAUSS))
        spread[3] = growth
        growth = growth * growth
        spread[4] = growth
        spread[5] = growth * growth
        levels[...] = values[part].reshape(rows, visible) * wave

    def wide(ref, i):
        return jnp.broadcast_to(ref[i : i + 1], (16, visible))

    def rows(ref, i, paired):
        near = wide(ref.at[1], i).astype(bf16)
        apart = wide(ref.at[2], i).astype(bf16)
        low = jnp.exp2(jnp.broadcast_to(ref[0, i : i + 1], (8, visible)) * lean)
        high = low * jnp.broadcast_to(ref[3, i : i + 1], (8, visible))
        rise = jnp.concatenate([low, high], 0).astype(bf16)
        growth = wide(ref.at[4], i).astype(bf16)
        result = []
        if not paired:
            for a in range(TILE // 16):
                result.append(rise * pl.reciprocal((spots[a] - near) - apart, approx=True))
                rise = rise * growth
            return result
        twice = wide(ref.at[5], i).astype(bf16)
        for a in range(0, TILE // 16, 2):
            here = (spots[a] - near) - apart
            next = (spots[a + 1] - near) - apart
            ratio = rise * pl.reciprocal(here * next, approx=True)
            result += [ratio * next, (ratio * growth) * here]
            rise = rise * twice
        return result

    def several(b, carry):
        for load in loads(b):
            load.wait()
        prepare(b)
        for i in range(JOINT):
            along = jnp.concatenate(rows(spread, 2 * i, True), 0)
            down = rows(spread, 2 * i + 1, False)
            right = []
            for c in range(2):
                level = wide(levels, 2 * i + c).astype(bf16)
                right += [d * level for d in down]
            patch = lax.dot_general(
                along, jnp.concatenate(right, 0), (((1,), (1,)), ((), ())), preferred_element_type=f32
            )
            k = b * JOINT + i
            sums[k + 1] = sums[links[0, k]] + patch
        return carry

    link_load.wait()
    lax.fori_loop(0, steps, several, 0)

    down = lax.broadcasted_iota(jnp.int32, (TILE, 2 * TILE), 0) - MIDDLE
    along = lax.broadcasted_iota(jnp.int32, (TILE, 2 * TILE), 1) % TILE - MIDDLE
    power = (down * down + along * along).astype(jnp.float32)
    flip = 1.0 - 2.0 * ((down + along + 2 * TILE) % 2).astype(jnp.float32)
    fall = flip * jnp.exp2(power * -GAUSS)
    for a in range(SUB // TILE):
        for e in range(SUB // TILE):
            spot = (slice(a * TILE, (a + 1) * TILE), slice(e * 2 * TILE, (e + 1) * 2 * TILE))
            part[spot] = (sums[links[1, a * (SUB // TILE) + e]] * fall).astype(bf16)
    for load in tables:
        load.wait()
    both = []
    for g in range(groups):
        image = jnp.dot(
            part[...], col[:, 2 * LANES * g : 2 * LANES * (g + 1)], preferred_element_type=f32
        )
        image = (image * unitary).astype(bf16)
        both.append(jnp.concatenate([image[:, :LANES], image[:, LANES:]], 0))

    def transformed(which, target):
        rows = table[pl.ds(pl.multiple_of(which * (SUB // 2), SUB // 2), SUB // 2)]
        for g in range(groups):
            result = jnp.dot(rows, both[g], preferred_element_type=f32)
            result = (result * unitary).astype(bf16)
            target[NBLK * g : NBLK * (g + 1)] = result.reshape(NBLK, half, LANES)

    share = pltpu.make_async_remote_copy(
        src_ref=lent, dst_ref=borrowed, send_sem=share_sem.at[0], recv_sem=share_sem.at[1],
        device_id=mate, device_id_type=MESH,
    )

    def scatter(peer):
        return pltpu.make_async_remote_copy(
            src_ref=spectra.at[peer[0]], dst_ref=pieces.at[me_g * pairs + side],
            send_sem=send1, recv_sem=recv1, device_id=peer, device_id_type=MESH,
        )

    gather = pltpu.make_async_remote_copy(
        src_ref=gathered.at[0], dst_ref=gathered.at[1], send_sem=gather_sem.at[0],
        recv_sem=gather_sem.at[1], device_id=mate, device_id_type=MESH,
    )

    transformed(1 - core, lent)
    pl.semaphore_wait(barrier, len(greeted))
    share.start()
    transformed(core, spectra)
    share.wait_recv()
    spectra[...] = (spectra[...].astype(f32) + borrowed[...].astype(f32)).astype(bf16)
    for peer in peers:
        scatter(peer).start()
    pieces[me_g * pairs + side] = spectra[me_g]
    others = pieces.at[pl.ds(0, len(peers))]
    pltpu.make_async_copy(others, others, recv1).wait()
    whole = pieces[...].reshape(grid_count, pairs, half, LANES).astype(f32)
    gathered[0] = jnp.sum(whole, 1).astype(bf16)
    gather.start()
    sign = jnp.where(lax.broadcasted_iota(jnp.int32, (1, LANES), 1) < CONTRIB, -1.0, 1.0)

    def mixed(h, g):
        straight = gathered[h, NBLK * g : NBLK * (g + 1)].reshape(SUB // 2, LANES)
        turned = pltpu.roll(straight.astype(f32), CONTRIB, 1) * sign
        both = jnp.concatenate([straight, turned.astype(bf16)], 0)
        return jnp.dot(embed[h], both, preferred_element_type=f32)

    mixture = [mixed(0, g) for g in range(groups)]
    gather.wait_recv()
    for g in range(groups):
        result = mixture[g] + mixed(1, g)
        out[:, LANES * g : LANES * (g + 1)] = (result * scale[...]).astype(bf16)
    share.wait_send()
    pltpu.make_async_copy(others, others, send1).wait()
    gather.wait_send()


def image_kernel(mixture, table, weight, out, image, save_sem):
    rows_here = mixture.shape[0]
    saves = []
    for c in range(2):
        for h in range(SAVES):
            part = slice(h * (rows_here // SAVES), (h + 1) * (rows_here // SAVES))
            result = jnp.dot(
                mixture[part], table[:, c * FAC : (c + 1) * FAC], preferred_element_type=jnp.float32
            )
            image[c, part] = result * weight[...]
            saves.append(
                pltpu.make_async_copy(
                    image.at[c, part], out.at[0, c, part], save_sem.at[c * SAVES + h]
                )
            )
            saves[-1].start()
    for save in saves:
        save.wait()


def shards(grid_count, vis_count, vis_coords, vis_values, tile_index):
    groups = grid_count // NBLK
    half = CONTRIB // 2
    rows_here = FAC // vis_count
    unitary = 1.0 / math.sqrt(SUB)
    bf16, f32 = jnp.bfloat16, jnp.float32
    far = pl.BlockSpec(memory_space=pltpu.HBM)
    inside = pl.BlockSpec(memory_space=pltpu.VMEM)
    dma = pltpu.SemaphoreType.DMA
    blocks = vis_coords.shape[1]
    visible = vis_coords.shape[3]
    row_scale = taper() * (unitary / math.sqrt(CONTRIB * groups))
    row_scale = np.broadcast_to(row_scale[:, None], (FAC, LANES)).astype(np.float32)
    mixture = pl.pallas_call(
        functools.partial(subgrid_kernel, grid_count, vis_count, unitary),
        out_shape=jax.ShapeDtypeStruct((rows_here, groups * LANES), bf16),
        in_specs=[far] * 7,
        out_specs=inside,
        scratch_shapes=[
            pltpu.VMEM((1, blocks), jnp.int32),
            pltpu.VMEM((2, LANES), jnp.int32),
            pltpu.SMEM((2, LANES), jnp.int32),
            pltpu.VMEM((blocks, 2, visible), f32),
            pltpu.VMEM((blocks, 2, visible), f32),
            pltpu.VMEM((2 * JOINT, visible), f32),
            pltpu.VMEM((6, 2 * JOINT, visible), f32),
            pltpu.VMEM((blocks + 1, TILE, 2 * TILE), f32),
            pltpu.VMEM((2 * SUB, 2 * LANES * groups), bf16),
            pltpu.VMEM((SUB, 2 * SUB), bf16),
            pltpu.VMEM((2, rows_here, SUB), bf16),
            pltpu.VMEM((rows_here, LANES), f32),
            pltpu.VMEM((SUB, 2 * SUB), bf16),
            pltpu.VMEM((grid_count, half, LANES), bf16),
            pltpu.VMEM((grid_count, half, LANES), bf16),
            pltpu.VMEM((grid_count, half, LANES), bf16),
            pltpu.VMEM((grid_count * vis_count // 2, half, LANES), bf16),
            pltpu.VMEM((2, grid_count, half, LANES), bf16),
            dma,
            dma,
            dma((blocks // JOINT, 2)),
            dma((5,)),
            dma((2,)),
            dma((2,)),
            dma,
            dma,
        ],
        compiler_params=pltpu.CompilerParams(
            collective_id=0, has_side_effects=True, vmem_limit_bytes=ROOM
        ),
        cost_estimate=pl.CostEstimate(flops=10**10, bytes_accessed=10**6, transcendentals=10**6),
        name="subgrids",
    )(
        *[
            pltpu.with_memory_space_constraint(array, pltpu.HBM)
            for array in (
                tile_index,
                vis_coords.reshape(blocks, 2, visible),
                vis_values.reshape(blocks, 2, visible),
                jnp.asarray(column_table(groups)),
                jnp.asarray(row_table()),
                jnp.asarray(embed_table()),
                jnp.asarray(row_scale),
            )
        ]
    )

    return pl.pallas_call(
        image_kernel,
        out_shape=jax.ShapeDtypeStruct((1, 2, rows_here, FAC), f32),
        in_specs=[inside] * 3,
        out_specs=far,
        scratch_shapes=[pltpu.VMEM((2, rows_here, FAC), f32), dma((2 * SAVES,))],
        compiler_params=pltpu.CompilerParams(vmem_limit_bytes=ROOM),
        name="images",
    )(
        mixture,
        jnp.asarray(output_table(groups)),
        jnp.asarray(taper()[None, :].astype(np.float32)),
    )


def solution(mesh):
    placed = (P("grid", "vis", None, None), P("grid", "vis", None, None), P("grid", "vis"))
    body = functools.partial(shards, mesh.shape["grid"], mesh.shape["vis"])
    return jax.shard_map(
        body, mesh=mesh, in_specs=placed, out_specs=P("grid", None, "vis", None), check_vma=False
    )
```

```python
import functools
import math

import jax
import jax.numpy as jnp
import ml_dtypes
import numpy as np
from jax import lax
from jax.experimental import pallas as pl
from jax.experimental.pallas import tpu as pltpu
from jax.sharding import PartitionSpec as P

SUB = 512
FAC = 1024
CONTRIB = 64
TILE = 64
NBLK = 8
LANES = 2 * CONTRIB
TAPER_SCALE = 16.0
SAVES = 4
WAVES = 2
JOINT = 32
SPLIT = 2
ROOM = 32 * 2**20
MESH = pl.DeviceIdType.MESH


def phase_pair(frequencies, points, length):
    phases = (frequencies[:, None] * points[None, :]) % length
    angles = phases * (2.0 * math.pi / length)
    return np.cos(angles).astype(np.float32), np.sin(angles).astype(np.float32)


def as_bf16(array):
    return array.astype(ml_dtypes.bfloat16)


def column_table(groups):
    cos, sin = phase_pair(np.arange(SUB), np.arange(groups * CONTRIB), SUB)
    across = SUB // TILE
    table = np.zeros((across, 2, TILE, groups, 4, CONTRIB), np.float32)
    cos = cos.reshape(across, TILE, groups, CONTRIB)
    sin = sin.reshape(across, TILE, groups, CONTRIB)
    table[:, 0, :, :, 0], table[:, 1, :, :, 0] = cos, sin
    table[:, 0, :, :, 1], table[:, 1, :, :, 1] = -sin, cos
    table[:, :, :, :, 2] = -table[:, :, :, :, 1]
    table[:, :, :, :, 3] = table[:, :, :, :, 0]
    return as_bf16(table.reshape(2 * SUB, groups * 4 * CONTRIB))


def row_table():
    order = np.arange(SUB).reshape(NBLK, 2, CONTRIB // 2).transpose(1, 0, 2).reshape(SUB)
    cos, sin = phase_pair(order, np.arange(SUB), SUB)
    return as_bf16(np.concatenate([cos, -sin], 1))


def embed_table(unit):
    order = np.arange(SUB).reshape(NBLK // unit, unit, 2, CONTRIB // 2).transpose(2, 0, 1, 3)
    order = order.reshape(2, NBLK // unit, -1)
    cos, sin = phase_pair(np.arange(FAC), order.reshape(-1), FAC)
    parts = np.stack([part.reshape(FAC, *order.shape) for part in (cos, sin)], 3)
    return as_bf16(parts.transpose(1, 0, 2, 3, 4).reshape(2, FAC, SUB))


def output_table(groups):
    cos, sin = phase_pair(np.arange(groups * CONTRIB), np.arange(FAC), FAC)
    cos = cos.reshape(groups, CONTRIB, FAC)
    sin = sin.reshape(groups, CONTRIB, FAC)
    real = np.stack([cos, -sin], 1).reshape(groups * LANES, FAC)
    imag = np.stack([sin, cos], 1).reshape(groups * LANES, FAC)
    return as_bf16(np.concatenate([real, imag], 1))


def taper():
    sines = np.sin(np.pi * (np.arange(FAC) + 0.5) / FAC)
    return 0.25 + 0.75 * sines * sines


SINE = [(-1.0) ** k * math.pi ** (2 * k) / math.factorial(2 * k + 1) for k in range(7)]


GAUSS = math.log2(math.e) / (TAPER_SCALE * TAPER_SCALE)
MIDDLE = TILE // 2


def swapped(index, bits):
    result = index
    bit = 1
    while bit <= bits:
        if bits & bit:
            result = result + bit * (1 - 2 * ((index // bit) % 2))
        bit *= 2
    return result


def chains(tile_row, chain):
    blocks = tile_row.shape[1]
    across = jnp.broadcast_to(tile_row[...], (blocks, blocks))
    down = across.T
    above = lax.broadcasted_iota(jnp.int32, (blocks, blocks), 0)
    beside = lax.broadcasted_iota(jnp.int32, (blocks, blocks), 1)
    before = jnp.where((across == down) & (above < beside), above + 1, 0)
    latest = jnp.where(down == beside, above + 1, 0)
    for k, table in enumerate((before, latest)):
        while table.shape[0] > 8:
            half = table.shape[0] // 2
            table = jnp.maximum(table[:half], table[half:])
        for turn in (4, 2, 1):
            table = jnp.maximum(table, pltpu.roll(table, turn, 0))
        chain[k : k + 1, :blocks] = table[:1]


def subgrid_kernel(
    grid_count, vis_count, unitary,
    tiles_hbm, coords_hbm, values_hbm, col_hbm, row_hbm, embed_hbm, scale_hbm, out,
    tile_row, chain, links, coords, values, levels, spread, sums,
    col, table, embed, scale, part, lent, borrowed, spectra, pieces, gathered,
    tile_sem, link_sem, visible_sem, load_sem, share_sem, gather_sem, send1, recv1,
):
    me_g, me_v = lax.axis_index("grid"), lax.axis_index("vis")
    groups = grid_count // NBLK
    rows_here = out.shape[0]
    half = CONTRIB // 2
    size = grid_count // WAVES
    unit = min(NBLK, size)
    mine = pl.ds(pl.multiple_of(me_v * rows_here, rows_here), rows_here)
    blocks, visible = tile_row.shape[1], coords.shape[0] * LANES // (2 * tile_row.shape[1])
    tall = 2 * visible // LANES
    f32, bf16 = jnp.float32, jnp.bfloat16
    steps = blocks // JOINT

    def loads(i):
        part = pl.ds(i * JOINT * tall, JOINT * tall)
        return (
            pltpu.make_async_copy(coords_hbm.at[part], coords.at[part], visible_sem.at[i, 0]),
            pltpu.make_async_copy(values_hbm.at[part], values.at[part], visible_sem.at[i, 1]),
        )

    tile_load = pltpu.make_async_copy(tiles_hbm, tile_row, tile_sem)
    tile_load.start()
    for i in range(steps):
        for load in loads(i):
            load.start()
    pairs = vis_count // 2
    core, side = me_v % 2, me_v // 2
    mate = (me_g, swapped(me_v, 1))
    peers = [
        (swapped(me_g, g), swapped(me_v, 2 * x))
        for g in range(grid_count - 1, -1, -1)
        for x in range(pairs - 1, -1, -1)
        if g or x
    ]
    barrier = pltpu.get_barrier_semaphore()
    greeted = peers + [mate]
    for peer in greeted:
        pl.semaphore_signal(barrier, inc=1, device_id=peer, device_id_type=MESH)
    tables = [
        pltpu.make_async_copy(col_hbm, col, load_sem.at[0]),
        pltpu.make_async_copy(row_hbm, table, load_sem.at[1]),
        pltpu.make_async_copy(embed_hbm.at[core, mine], embed.at[0], load_sem.at[2]),
        pltpu.make_async_copy(embed_hbm.at[1 - core, mine], embed.at[1], load_sem.at[3]),
        pltpu.make_async_copy(scale_hbm.at[mine], scale, load_sem.at[4]),
    ]
    for load in tables:
        load.start()
    sums[0] = jnp.zeros((TILE, 2 * TILE), f32)
    tile_load.wait()
    chains(tile_row, chain)
    link_load = pltpu.make_async_copy(chain, links, link_sem)
    link_load.start()
    row = lax.broadcasted_iota(jnp.int32, (16, 1), 0).astype(f32)
    lean = (row[:8] - MIDDLE) * (2.0 * GAUSS)
    width = visible // SPLIT
    spots = [
        jnp.broadcast_to((row + 16.0 * a).astype(bf16), (16, width)) for a in range(TILE // 16)
    ]
    even = lax.broadcasted_iota(jnp.int32, (JOINT * tall, LANES), 0) % 2 == 0

    def prepare(b):
        part = pl.ds(b * JOINT * tall, JOINT * tall)
        where = coords[part]
        nearest = jnp.floor(where + 0.5)
        offset = where - nearest
        offset = jnp.where(jnp.abs(offset) < 1e-10, 1e-10, offset)
        square = offset * offset
        wave = square * SINE[5] + SINE[4]
        for k in range(3, -1, -1):
            wave = wave * square + SINE[k]
        half = nearest * 0.5
        odd = (half - jnp.floor(half)) * 4.0 - 1.0
        centred = where - MIDDLE
        wave = (wave * offset) * (odd * jnp.exp2(centred * centred * -GAUSS))
        rows = JOINT * tall
        wave = wave * jnp.where(even, pltpu.roll(wave, rows - 1, 0), pltpu.roll(wave, 1, 0))
        spread[0] = centred
        spread[1] = nearest
        spread[2] = offset
        growth = jnp.exp2(centred * (16.0 * GAUSS))
        spread[3] = growth
        growth = growth * growth
        spread[4] = growth
        levels[...] = values[part] * wave

    def spread_out(ref, i, count):
        rows = [
            jnp.broadcast_to(ref[i + 2 * t : i + 2 * t + 1], (count, LANES))
            for t in range(width // LANES)
        ]
        return jnp.concatenate(rows, 1)

    def wide(ref, i):
        return spread_out(ref, i, 16).astype(bf16)

    def rows(i, paired):
        near = wide(spread.at[1], i)
        apart = wide(spread.at[2], i)
        low = jnp.exp2(spread_out(spread.at[0], i, 8) * lean)
        high = low * spread_out(spread.at[3], i, 8)
        rise = jnp.concatenate([low, high], 0).astype(bf16)
        growth = wide(spread.at[4], i)
        result = []
        if not paired:
            for a in range(TILE // 16):
                result.append(rise * pl.reciprocal((spots[a] - near) - apart, approx=True))
                rise = rise * growth
            return result
        twice = growth * growth
        for a in range(0, TILE // 16, 2):
            here = (spots[a] - near) - apart
            next = (spots[a + 1] - near) - apart
            ratio = rise * pl.reciprocal(here * next, approx=True)
            result += [ratio * next, (ratio * growth) * here]
            rise = rise * twice
        return result

    def piece(i):
        down = rows(i + 1, False)
        right = []
        for c in range(2):
            level = wide(levels, i + c)
            right += [d * level for d in down]
        right = jnp.concatenate(right, 0)
        along = jnp.concatenate(rows(i, False), 0)
        return lax.dot_general(
            along, right, (((1,), (1,)), ((), ())), preferred_element_type=f32
        )

    def several(b, carry):
        for load in loads(b):
            load.wait()
        prepare(b)

        @pl.when(b == 0)
        def _():
            link_load.wait()

        for i in range(JOINT):
            k = b * JOINT + i
            patch = sums[links[0, k]]
            for h in range(SPLIT):
                patch = patch + piece(i * tall + h * (tall // SPLIT))
            sums[k + 1] = patch
        return carry

    lax.fori_loop(0, steps, several, 0)

    down = lax.broadcasted_iota(jnp.int32, (TILE, 2 * TILE), 0) - MIDDLE
    along = lax.broadcasted_iota(jnp.int32, (TILE, 2 * TILE), 1) % TILE - MIDDLE
    power = (down * down + along * along).astype(jnp.float32)
    flip = 1.0 - 2.0 * ((down + along + 2 * TILE) % 2).astype(jnp.float32)
    fall = flip * jnp.exp2(power * -GAUSS)
    for a in range(SUB // TILE):
        for e in range(SUB // TILE):
            spot = (slice(a * TILE, (a + 1) * TILE), slice(e * 2 * TILE, (e + 1) * 2 * TILE))
            part[spot] = (sums[links[1, a * (SUB // TILE) + e]] * fall).astype(bf16)
    for load in tables[:2]:
        load.wait()
    both = []
    for g in range(groups):
        image = jnp.dot(
            part[...], col[:, 2 * LANES * g : 2 * LANES * (g + 1)], preferred_element_type=f32
        )
        image = (image * unitary).astype(bf16)
        both.append(jnp.concatenate([image[:, :LANES], image[:, LANES:]], 0))

    def transformed(which, target):
        rows = table[pl.ds(pl.multiple_of(which * (SUB // 2), SUB // 2), SUB // 2)]
        for g in range(groups):
            result = jnp.dot(rows, both[g], preferred_element_type=f32)
            result = (result * unitary).astype(bf16)
            target[NBLK * g : NBLK * (g + 1)] = result.reshape(NBLK, half, LANES)

    share = pltpu.make_async_remote_copy(
        src_ref=lent, dst_ref=borrowed, send_sem=share_sem.at[0], recv_sem=share_sem.at[1],
        device_id=mate, device_id_type=MESH,
    )

    def scatter(peer):
        return pltpu.make_async_remote_copy(
            src_ref=spectra.at[peer[0]], dst_ref=pieces.at[me_g * pairs + side],
            send_sem=send1, recv_sem=recv1.at[me_g // size], device_id=peer, device_id_type=MESH,
        )

    def gather(w):
        return pltpu.make_async_remote_copy(
            src_ref=gathered.at[w, 0], dst_ref=gathered.at[w, 1], send_sem=gather_sem.at[w, 0],
            recv_sem=gather_sem.at[w, 1], device_id=mate, device_id_type=MESH,
        )

    transformed(1 - core, lent)
    pl.semaphore_wait(barrier, len(greeted))
    share.start()
    transformed(core, spectra)
    share.wait_recv()
    spectra[...] = (spectra[...].astype(f32) + borrowed[...].astype(f32)).astype(bf16)
    for peer in peers:
        scatter(peer).start()
    own = pltpu.make_async_copy(
        spectra.at[me_g], pieces.at[me_g * pairs + side], recv1.at[me_g // size]
    )
    own.start()
    for load in tables[2:]:
        load.wait()
    sign = jnp.where(lax.broadcasted_iota(jnp.int32, (1, LANES), 1) < CONTRIB, -1.0, 1.0)
    mixture = [None] * groups

    def mixed(w, h):
        for k in range(size // unit):
            first = w * size + k * unit
            straight = gathered[w, h, k * unit : (k + 1) * unit].reshape(unit * half, LANES)
            turned = pltpu.roll(straight.astype(f32), CONTRIB, 1) * sign
            both = jnp.concatenate([straight, turned.astype(bf16)], 0)
            at = first % NBLK * 2 * half
            result = jnp.dot(
                embed[h, :, at : at + 2 * half * unit], both, preferred_element_type=f32
            )
            g = first // NBLK
            mixture[g] = result if mixture[g] is None else mixture[g] + result

    for w in range(WAVES):
        arrived = pieces.at[pl.ds(w * size * pairs, size * pairs)]
        pltpu.make_async_copy(arrived, arrived, recv1.at[w]).wait()
        whole = arrived[...].reshape(size, pairs, half, LANES).astype(f32)
        gathered[w, 0] = jnp.sum(whole, 1).astype(bf16)
        gather(w).start()
        mixed(w, 0)
        if w > 0:
            gather(w - 1).wait_recv()
            mixed(w - 1, 1)
    gather(WAVES - 1).wait_recv()
    mixed(WAVES - 1, 1)
    for g in range(groups):
        out[:, LANES * g : LANES * (g + 1)] = (mixture[g] * scale[...]).astype(bf16)
    share.wait_send()
    others = pieces.at[pl.ds(0, len(peers))]
    pltpu.make_async_copy(others, others, send1).wait()
    for w in range(WAVES):
        gather(w).wait_send()


def image_kernel(mixture, table, weight, out, image, save_sem):
    rows_here = mixture.shape[0]
    saves = []
    for c in range(2):
        for h in range(SAVES):
            part = slice(h * (rows_here // SAVES), (h + 1) * (rows_here // SAVES))
            result = jnp.dot(
                mixture[part], table[:, c * FAC : (c + 1) * FAC], preferred_element_type=jnp.float32
            )
            image[c, part] = result * weight[...]
            saves.append(
                pltpu.make_async_copy(
                    image.at[c, part], out.at[0, c, part], save_sem.at[c * SAVES + h]
                )
            )
            saves[-1].start()
    for save in saves:
        save.wait()


def shards(grid_count, vis_count, vis_coords, vis_values, tile_index):
    groups = grid_count // NBLK
    half = CONTRIB // 2
    rows_here = FAC // vis_count
    unitary = 1.0 / math.sqrt(SUB)
    bf16, f32 = jnp.bfloat16, jnp.float32
    far = pl.BlockSpec(memory_space=pltpu.HBM)
    inside = pl.BlockSpec(memory_space=pltpu.VMEM)
    dma = pltpu.SemaphoreType.DMA
    blocks = vis_coords.shape[1]
    visible = vis_coords.shape[3]
    tall = 2 * visible // LANES

    def tiled(array):
        array = array.reshape(blocks, 2, visible // LANES, LANES)
        return array.transpose(0, 2, 1, 3).reshape(blocks * tall, LANES)

    row_scale = taper() * (unitary / math.sqrt(CONTRIB * groups))
    row_scale = np.broadcast_to(row_scale[:, None], (FAC, LANES)).astype(np.float32)
    mixture = pl.pallas_call(
        functools.partial(subgrid_kernel, grid_count, vis_count, unitary),
        out_shape=jax.ShapeDtypeStruct((rows_here, groups * LANES), bf16),
        in_specs=[far] * 7,
        out_specs=inside,
        scratch_shapes=[
            pltpu.VMEM((1, blocks), jnp.int32),
            pltpu.VMEM((2, LANES), jnp.int32),
            pltpu.SMEM((2, LANES), jnp.int32),
            pltpu.VMEM((blocks * tall, LANES), f32),
            pltpu.VMEM((blocks * tall, LANES), f32),
            pltpu.VMEM((JOINT * tall, LANES), f32),
            pltpu.VMEM((5, JOINT * tall, LANES), f32),
            pltpu.VMEM((blocks + 1, TILE, 2 * TILE), f32),
            pltpu.VMEM((2 * SUB, 2 * LANES * groups), bf16),
            pltpu.VMEM((SUB, 2 * SUB), bf16),
            pltpu.VMEM((2, rows_here, SUB), bf16),
            pltpu.VMEM((rows_here, LANES), f32),
            pltpu.VMEM((SUB, 2 * SUB), bf16),
            pltpu.VMEM((grid_count, half, LANES), bf16),
            pltpu.VMEM((grid_count, half, LANES), bf16),
            pltpu.VMEM((grid_count, half, LANES), bf16),
            pltpu.VMEM((grid_count * vis_count // 2, half, LANES), bf16),
            pltpu.VMEM((WAVES, 2, grid_count // WAVES, half, LANES), bf16),
            dma,
            dma,
            dma((blocks // JOINT, 2)),
            dma((5,)),
            dma((2,)),
            dma((WAVES, 2)),
            dma,
            dma((WAVES,)),
        ],
        compiler_params=pltpu.CompilerParams(
            collective_id=0, has_side_effects=True, vmem_limit_bytes=ROOM
        ),
        cost_estimate=pl.CostEstimate(flops=10**10, bytes_accessed=10**6, transcendentals=10**6),
        name="subgrids",
    )(
        *[
            pltpu.with_memory_space_constraint(array, pltpu.HBM)
            for array in (
                tile_index,
                tiled(vis_coords),
                tiled(vis_values),
                jnp.asarray(column_table(groups)),
                jnp.asarray(row_table()),
                jnp.asarray(embed_table(min(NBLK, grid_count // WAVES))),
                jnp.asarray(row_scale),
            )
        ]
    )

    return pl.pallas_call(
        image_kernel,
        out_shape=jax.ShapeDtypeStruct((1, 2, rows_here, FAC), f32),
        in_specs=[inside] * 3,
        out_specs=far,
        scratch_shapes=[pltpu.VMEM((2, rows_here, FAC), f32), dma((2 * SAVES,))],
        compiler_params=pltpu.CompilerParams(vmem_limit_bytes=ROOM),
        name="images",
    )(
        mixture,
        jnp.asarray(output_table(groups)),
        jnp.asarray(taper()[None, :].astype(np.float32)),
    )


def solution(mesh):
    placed = (P("grid", "vis", None, None), P("grid", "vis", None, None), P("grid", "vis"))
    body = functools.partial(shards, mesh.shape["grid"], mesh.shape["vis"])
    return jax.shard_map(
        body, mesh=mesh, in_specs=placed, out_specs=P("grid", None, "vis", None), check_vma=False
    )
```

```python
import functools
import math

import jax
import jax.numpy as jnp
import ml_dtypes
import numpy as np
from jax import lax
from jax.experimental import pallas as pl
from jax.experimental.pallas import tpu as pltpu
from jax.sharding import PartitionSpec as P

SUB = 512
FAC = 1024
CONTRIB = 64
TILE = 64
NBLK = 8
LANES = 2 * CONTRIB
TAPER_SCALE = 16.0
SAVES = 4
WAVES = 2
JOINT = 32
SPLIT = 2
ROOM = 32 * 2**20
MESH = pl.DeviceIdType.MESH


def phase_pair(frequencies, points, length):
    phases = (frequencies[:, None] * points[None, :]) % length
    angles = phases * (2.0 * math.pi / length)
    return np.cos(angles).astype(np.float32), np.sin(angles).astype(np.float32)


def as_bf16(array):
    return array.astype(ml_dtypes.bfloat16)


def column_table(groups):
    cos, sin = phase_pair(np.arange(SUB), np.arange(groups * CONTRIB), SUB)
    across = SUB // TILE
    table = np.zeros((across, 2, TILE, groups, 4, CONTRIB), np.float32)
    cos = cos.reshape(across, TILE, groups, CONTRIB)
    sin = sin.reshape(across, TILE, groups, CONTRIB)
    table[:, 0, :, :, 0], table[:, 1, :, :, 0] = cos, sin
    table[:, 0, :, :, 1], table[:, 1, :, :, 1] = -sin, cos
    table[:, :, :, :, 2] = -table[:, :, :, :, 1]
    table[:, :, :, :, 3] = table[:, :, :, :, 0]
    return as_bf16(table.reshape(2 * SUB, groups * 4 * CONTRIB))


def row_table():
    order = np.arange(SUB).reshape(NBLK, 2, CONTRIB // 2).transpose(1, 0, 2).reshape(SUB)
    cos, sin = phase_pair(order, np.arange(SUB), SUB)
    return as_bf16(np.concatenate([cos, -sin], 1))


def embed_table(unit):
    order = np.arange(SUB).reshape(NBLK // unit, unit, 2, CONTRIB // 2).transpose(2, 0, 1, 3)
    order = order.reshape(2, NBLK // unit, -1)
    cos, sin = phase_pair(np.arange(FAC), order.reshape(-1), FAC)
    parts = np.stack([part.reshape(FAC, *order.shape) for part in (cos, sin)], 3)
    return as_bf16(parts.transpose(1, 0, 2, 3, 4).reshape(2, FAC, SUB))


def output_table(groups):
    cos, sin = phase_pair(np.arange(groups * CONTRIB), np.arange(FAC), FAC)
    cos = cos.reshape(groups, CONTRIB, FAC)
    sin = sin.reshape(groups, CONTRIB, FAC)
    real = np.stack([cos, -sin], 1).reshape(groups * LANES, FAC)
    imag = np.stack([sin, cos], 1).reshape(groups * LANES, FAC)
    return as_bf16(np.concatenate([real, imag], 1))


def taper():
    sines = np.sin(np.pi * (np.arange(FAC) + 0.5) / FAC)
    return 0.25 + 0.75 * sines * sines


SINE = [(-1.0) ** k * math.pi ** (2 * k) / math.factorial(2 * k + 1) for k in range(7)]


GAUSS = math.log2(math.e) / (TAPER_SCALE * TAPER_SCALE)
MIDDLE = TILE // 2


def swapped(index, bits):
    result = index
    bit = 1
    while bit <= bits:
        if bits & bit:
            result = result + bit * (1 - 2 * ((index // bit) % 2))
        bit *= 2
    return result


def chains(tile_row, chain):
    blocks = tile_row.shape[1]
    across = jnp.broadcast_to(tile_row[...], (blocks, blocks))
    down = across.T
    above = lax.broadcasted_iota(jnp.int32, (blocks, blocks), 0)
    beside = lax.broadcasted_iota(jnp.int32, (blocks, blocks), 1)
    before = jnp.where((across == down) & (above < beside), above + 1, 0)
    latest = jnp.where(down == beside, above + 1, 0)
    for k, table in enumerate((before, latest)):
        while table.shape[0] > 8:
            half = table.shape[0] // 2
            table = jnp.maximum(table[:half], table[half:])
        for turn in (4, 2, 1):
            table = jnp.maximum(table, pltpu.roll(table, turn, 0))
        chain[k : k + 1, :blocks] = table[:1]


def subgrid_kernel(
    grid_count, vis_count, unitary,
    tiles_hbm, coords_hbm, values_hbm, col_hbm, row_hbm, embed_hbm, scale_hbm, out,
    tile_row, chain, links, coords, values, levels, spread, sums,
    col, table, embed, scale, part, lent, borrowed, spectra, pieces, gathered,
    tile_sem, link_sem, visible_sem, load_sem, share_sem, gather_sem, send1, recv1,
):
    me_g, me_v = lax.axis_index("grid"), lax.axis_index("vis")
    groups = grid_count // NBLK
    rows_here = out.shape[0]
    half = CONTRIB // 2
    size = grid_count // WAVES
    unit = min(NBLK, size)
    mine = pl.ds(pl.multiple_of(me_v * rows_here, rows_here), rows_here)
    blocks, visible = tile_row.shape[1], coords.shape[0] * LANES // (2 * tile_row.shape[1])
    tall = 2 * visible // LANES
    f32, bf16 = jnp.float32, jnp.bfloat16
    steps = blocks // JOINT

    def loads(i):
        part = pl.ds(i * JOINT * tall, JOINT * tall)
        return (
            pltpu.make_async_copy(coords_hbm.at[part], coords.at[part], visible_sem.at[i, 0]),
            pltpu.make_async_copy(values_hbm.at[part], values.at[part], visible_sem.at[i, 1]),
        )

    for load in loads(0):
        load.start()
    tile_load = pltpu.make_async_copy(tiles_hbm, tile_row, tile_sem)
    tile_load.start()
    for i in range(1, steps):
        for load in loads(i):
            load.start()
    pairs = vis_count // 2
    core, side = me_v % 2, me_v // 2
    mate = (me_g, swapped(me_v, 1))
    chips = grid_count * pairs
    here = me_g * pairs + side
    peers = []
    for k in range(chips - 1):
        chip = k + (k - here + chips) // chips
        peers.append((chip // pairs, chip % pairs * 2 + core))
    barrier = pltpu.get_barrier_semaphore()
    greeted = peers + [mate]
    for peer in greeted:
        pl.semaphore_signal(barrier, inc=1, device_id=peer, device_id_type=MESH)
    tables = [
        pltpu.make_async_copy(col_hbm, col, load_sem.at[0]),
        pltpu.make_async_copy(row_hbm, table, load_sem.at[1]),
        pltpu.make_async_copy(embed_hbm.at[core, mine], embed.at[0], load_sem.at[2]),
        pltpu.make_async_copy(embed_hbm.at[1 - core, mine], embed.at[1], load_sem.at[3]),
        pltpu.make_async_copy(scale_hbm.at[mine], scale, load_sem.at[4]),
    ]
    for load in tables:
        load.start()
    sums[0] = jnp.zeros((TILE, 2 * TILE), f32)
    tile_load.wait()
    chains(tile_row, chain)
    link_load = pltpu.make_async_copy(chain, links, link_sem)
    link_load.start()
    row = lax.broadcasted_iota(jnp.int32, (16, 1), 0).astype(f32)
    lean = (row[:8] - MIDDLE) * (2.0 * GAUSS)
    width = visible // SPLIT
    spots = [
        jnp.broadcast_to((row + 16.0 * a).astype(bf16), (16, width)) for a in range(TILE // 16)
    ]
    even = lax.broadcasted_iota(jnp.int32, (JOINT * tall, LANES), 0) % 2 == 0

    def prepare(b):
        part = pl.ds(b * JOINT * tall, JOINT * tall)
        where = coords[part]
        nearest = jnp.floor(where + 0.5)
        offset = where - nearest
        offset = jnp.where(jnp.abs(offset) < 1e-10, 1e-10, offset)
        square = offset * offset
        wave = square * SINE[5] + SINE[4]
        for k in range(3, -1, -1):
            wave = wave * square + SINE[k]
        half = nearest * 0.5
        odd = (half - jnp.floor(half)) * 4.0 - 1.0
        centred = where - MIDDLE
        wave = (wave * offset) * (odd * jnp.exp2(centred * centred * -GAUSS))
        rows = JOINT * tall
        wave = wave * jnp.where(even, pltpu.roll(wave, rows - 1, 0), pltpu.roll(wave, 1, 0))
        spread[0] = centred
        spread[1] = nearest
        spread[2] = offset
        growth = jnp.exp2(centred * (16.0 * GAUSS))
        spread[3] = growth
        growth = growth * growth
        spread[4] = growth
        levels[...] = values[part] * wave

    def spread_out(ref, i, count):
        rows = [
            jnp.broadcast_to(ref[i + 2 * t : i + 2 * t + 1], (count, LANES))
            for t in range(width // LANES)
        ]
        return jnp.concatenate(rows, 1)

    def wide(ref, i):
        return spread_out(ref, i, 16).astype(bf16)

    def rows(i, paired):
        near = wide(spread.at[1], i)
        apart = wide(spread.at[2], i)
        low = jnp.exp2(spread_out(spread.at[0], i, 8) * lean)
        high = low * spread_out(spread.at[3], i, 8)
        rise = jnp.concatenate([low, high], 0).astype(bf16)
        growth = wide(spread.at[4], i)
        result = []
        if not paired:
            for a in range(TILE // 16):
                result.append(rise * pl.reciprocal((spots[a] - near) - apart, approx=True))
                rise = rise * growth
            return result
        twice = growth * growth
        for a in range(0, TILE // 16, 2):
            here = (spots[a] - near) - apart
            next = (spots[a + 1] - near) - apart
            ratio = rise * pl.reciprocal(here * next, approx=True)
            result += [ratio * next, (ratio * growth) * here]
            rise = rise * twice
        return result

    def piece(i):
        down = rows(i + 1, False)
        right = []
        for c in range(2):
            level = wide(levels, i + c)
            right += [d * level for d in down]
        right = jnp.concatenate(right, 0)
        along = jnp.concatenate(rows(i, False), 0)
        return lax.dot_general(
            along, right, (((1,), (1,)), ((), ())), preferred_element_type=f32
        )

    def several(b, carry):
        for load in loads(b):
            load.wait()
        prepare(b)

        @pl.when(b == 0)
        def _():
            link_load.wait()

        for i in range(JOINT):
            k = b * JOINT + i
            patch = sums[links[0, k]]
            for h in range(SPLIT):
                patch = patch + piece(i * tall + h * (tall // SPLIT))
            sums[k + 1] = patch
        return carry

    lax.fori_loop(0, steps, several, 0)

    down = lax.broadcasted_iota(jnp.int32, (TILE, 2 * TILE), 0) - MIDDLE
    along = lax.broadcasted_iota(jnp.int32, (TILE, 2 * TILE), 1) % TILE - MIDDLE
    power = (down * down + along * along).astype(jnp.float32)
    flip = 1.0 - 2.0 * ((down + along + 2 * TILE) % 2).astype(jnp.float32)
    fall = flip * jnp.exp2(power * -GAUSS)
    for a in range(SUB // TILE):
        for e in range(SUB // TILE):
            spot = (slice(a * TILE, (a + 1) * TILE), slice(e * 2 * TILE, (e + 1) * 2 * TILE))
            part[spot] = (sums[links[1, a * (SUB // TILE) + e]] * fall).astype(bf16)
    for load in tables[:2]:
        load.wait()
    both = []
    for g in range(groups):
        image = jnp.dot(
            part[...], col[:, 2 * LANES * g : 2 * LANES * (g + 1)], preferred_element_type=f32
        )
        image = (image * unitary).astype(bf16)
        both.append(jnp.concatenate([image[:, :LANES], image[:, LANES:]], 0))

    def transformed(which, target):
        rows = table[pl.ds(pl.multiple_of(which * (SUB // 2), SUB // 2), SUB // 2)]
        for g in range(groups):
            result = jnp.dot(rows, both[g], preferred_element_type=f32)
            result = (result * unitary).astype(bf16)
            target[NBLK * g : NBLK * (g + 1)] = result.reshape(NBLK, half, LANES)

    share = pltpu.make_async_remote_copy(
        src_ref=lent, dst_ref=borrowed, send_sem=share_sem.at[0], recv_sem=share_sem.at[1],
        device_id=mate, device_id_type=MESH,
    )

    def scatter(peer):
        return pltpu.make_async_remote_copy(
            src_ref=spectra.at[peer[0]], dst_ref=pieces.at[me_g * pairs + side],
            send_sem=send1, recv_sem=recv1.at[me_g // size], device_id=peer, device_id_type=MESH,
        )

    def gather(w):
        return pltpu.make_async_remote_copy(
            src_ref=gathered.at[w, 0], dst_ref=gathered.at[w, 1], send_sem=gather_sem.at[w, 0],
            recv_sem=gather_sem.at[w, 1], device_id=mate, device_id_type=MESH,
        )

    transformed(1 - core, lent)
    pl.semaphore_wait(barrier, len(greeted))
    share.start()
    transformed(core, spectra)
    share.wait_recv()
    spectra[...] = (spectra[...].astype(f32) + borrowed[...].astype(f32)).astype(bf16)
    for peer in peers:
        scatter(peer).start()
    own = pltpu.make_async_copy(
        spectra.at[me_g], pieces.at[me_g * pairs + side], recv1.at[me_g // size]
    )
    own.start()
    for load in tables[2:]:
        load.wait()
    sign = jnp.where(lax.broadcasted_iota(jnp.int32, (1, LANES), 1) < CONTRIB, -1.0, 1.0)
    mixture = [None] * groups

    def mixed(w, h):
        for k in range(size // unit):
            first = w * size + k * unit
            straight = gathered[w, h, k * unit : (k + 1) * unit].reshape(unit * half, LANES)
            turned = pltpu.roll(straight.astype(f32), CONTRIB, 1) * sign
            both = jnp.concatenate([straight, turned.astype(bf16)], 0)
            at = first % NBLK * 2 * half
            result = jnp.dot(
                embed[h, :, at : at + 2 * half * unit], both, preferred_element_type=f32
            )
            g = first // NBLK
            mixture[g] = result if mixture[g] is None else mixture[g] + result

    for w in range(WAVES):
        arrived = pieces.at[pl.ds(w * size * pairs, size * pairs)]
        pltpu.make_async_copy(arrived, arrived, recv1.at[w]).wait()
        whole = arrived[...].reshape(size, pairs, half, LANES).astype(f32)
        gathered[w, 0] = jnp.sum(whole, 1).astype(bf16)
        gather(w).start()
        mixed(w, 0)
        if w > 0:
            gather(w - 1).wait_recv()
            mixed(w - 1, 1)
    gather(WAVES - 1).wait_recv()
    mixed(WAVES - 1, 1)
    for g in range(groups):
        out[:, LANES * g : LANES * (g + 1)] = (mixture[g] * scale[...]).astype(bf16)
    share.wait_send()
    others = pieces.at[pl.ds(0, len(peers))]
    pltpu.make_async_copy(others, others, send1).wait()
    for w in range(WAVES):
        gather(w).wait_send()


def image_kernel(mixture, table, weight, out, image, save_sem):
    rows_here = mixture.shape[0]
    saves = []
    for c in range(2):
        for h in range(SAVES):
            part = slice(h * (rows_here // SAVES), (h + 1) * (rows_here // SAVES))
            result = jnp.dot(
                mixture[part], table[:, c * FAC : (c + 1) * FAC], preferred_element_type=jnp.float32
            )
            image[c, part] = result * weight[...]
            saves.append(
                pltpu.make_async_copy(
                    image.at[c, part], out.at[0, c, part], save_sem.at[c * SAVES + h]
                )
            )
            saves[-1].start()
    for save in saves:
        save.wait()


def shards(grid_count, vis_count, vis_coords, vis_values, tile_index):
    groups = grid_count // NBLK
    half = CONTRIB // 2
    rows_here = FAC // vis_count
    unitary = 1.0 / math.sqrt(SUB)
    bf16, f32 = jnp.bfloat16, jnp.float32
    far = pl.BlockSpec(memory_space=pltpu.HBM)
    inside = pl.BlockSpec(memory_space=pltpu.VMEM)
    dma = pltpu.SemaphoreType.DMA
    blocks = vis_coords.shape[1]
    visible = vis_coords.shape[3]
    tall = 2 * visible // LANES

    def tiled(array):
        array = array.reshape(blocks, 2, visible // LANES, LANES)
        return array.transpose(0, 2, 1, 3).reshape(blocks * tall, LANES)

    row_scale = taper() * (unitary / math.sqrt(CONTRIB * groups))
    row_scale = np.broadcast_to(row_scale[:, None], (FAC, LANES)).astype(np.float32)
    mixture = pl.pallas_call(
        functools.partial(subgrid_kernel, grid_count, vis_count, unitary),
        out_shape=jax.ShapeDtypeStruct((rows_here, groups * LANES), bf16),
        in_specs=[far] * 7,
        out_specs=inside,
        scratch_shapes=[
            pltpu.VMEM((1, blocks), jnp.int32),
            pltpu.VMEM((2, LANES), jnp.int32),
            pltpu.SMEM((2, LANES), jnp.int32),
            pltpu.VMEM((blocks * tall, LANES), f32),
            pltpu.VMEM((blocks * tall, LANES), f32),
            pltpu.VMEM((JOINT * tall, LANES), f32),
            pltpu.VMEM((5, JOINT * tall, LANES), f32),
            pltpu.VMEM((blocks + 1, TILE, 2 * TILE), f32),
            pltpu.VMEM((2 * SUB, 2 * LANES * groups), bf16),
            pltpu.VMEM((SUB, 2 * SUB), bf16),
            pltpu.VMEM((2, rows_here, SUB), bf16),
            pltpu.VMEM((rows_here, LANES), f32),
            pltpu.VMEM((SUB, 2 * SUB), bf16),
            pltpu.VMEM((grid_count, half, LANES), bf16),
            pltpu.VMEM((grid_count, half, LANES), bf16),
            pltpu.VMEM((grid_count, half, LANES), bf16),
            pltpu.VMEM((grid_count * vis_count // 2, half, LANES), bf16),
            pltpu.VMEM((WAVES, 2, grid_count // WAVES, half, LANES), bf16),
            dma,
            dma,
            dma((blocks // JOINT, 2)),
            dma((5,)),
            dma((2,)),
            dma((WAVES, 2)),
            dma,
            dma((WAVES,)),
        ],
        compiler_params=pltpu.CompilerParams(
            collective_id=0, has_side_effects=True, vmem_limit_bytes=ROOM
        ),
        cost_estimate=pl.CostEstimate(flops=10**10, bytes_accessed=10**6, transcendentals=10**6),
        name="subgrids",
    )(
        *[
            pltpu.with_memory_space_constraint(array, pltpu.HBM)
            for array in (
                tile_index,
                tiled(vis_coords),
                tiled(vis_values),
                jnp.asarray(column_table(groups)),
                jnp.asarray(row_table()),
                jnp.asarray(embed_table(min(NBLK, grid_count // WAVES))),
                jnp.asarray(row_scale),
            )
        ]
    )

    return pl.pallas_call(
        image_kernel,
        out_shape=jax.ShapeDtypeStruct((1, 2, rows_here, FAC), f32),
        in_specs=[inside] * 3,
        out_specs=far,
        scratch_shapes=[pltpu.VMEM((2, rows_here, FAC), f32), dma((2 * SAVES,))],
        compiler_params=pltpu.CompilerParams(vmem_limit_bytes=ROOM),
        name="images",
    )(
        mixture,
        jnp.asarray(output_table(groups)),
        jnp.asarray(taper()[None, :].astype(np.float32)),
    )


def solution(mesh):
    placed = (P("grid", "vis", None, None), P("grid", "vis", None, None), P("grid", "vis"))
    body = functools.partial(shards, mesh.shape["grid"], mesh.shape["vis"])
    return jax.shard_map(
        body, mesh=mesh, in_specs=placed, out_specs=P("grid", None, "vis", None), check_vma=False
    )
```

```python
import functools
import math

import jax
import jax.numpy as jnp
import ml_dtypes
import numpy as np
from jax import lax
from jax.experimental import pallas as pl
from jax.experimental.pallas import tpu as pltpu
from jax.sharding import PartitionSpec as P

SUB = 512
FAC = 1024
CONTRIB = 64
TILE = 64
NBLK = 8
LANES = 2 * CONTRIB
TAPER_SCALE = 16.0
SAVES = 4
WAVES = 1
JOINT = 32
SPLIT = 2
ROOM = 32 * 2**20
MESH = pl.DeviceIdType.MESH


def phase_pair(frequencies, points, length):
    phases = (frequencies[:, None] * points[None, :]) % length
    angles = phases * (2.0 * math.pi / length)
    return np.cos(angles).astype(np.float32), np.sin(angles).astype(np.float32)


def as_bf16(array):
    return array.astype(ml_dtypes.bfloat16)


def column_table(groups):
    cos, sin = phase_pair(np.arange(SUB), np.arange(groups * CONTRIB), SUB)
    across = SUB // TILE
    table = np.zeros((across, 2, TILE, groups, 4, CONTRIB), np.float32)
    cos = cos.reshape(across, TILE, groups, CONTRIB)
    sin = sin.reshape(across, TILE, groups, CONTRIB)
    table[:, 0, :, :, 0], table[:, 1, :, :, 0] = cos, sin
    table[:, 0, :, :, 1], table[:, 1, :, :, 1] = -sin, cos
    table[:, :, :, :, 2] = -table[:, :, :, :, 1]
    table[:, :, :, :, 3] = table[:, :, :, :, 0]
    return as_bf16(table.reshape(2 * SUB, groups * 4 * CONTRIB))


def row_table():
    order = np.arange(SUB).reshape(NBLK, 2, CONTRIB // 2).transpose(1, 0, 2).reshape(SUB)
    cos, sin = phase_pair(order, np.arange(SUB), SUB)
    return as_bf16(np.concatenate([cos, -sin], 1))


def embed_table(unit):
    order = np.arange(SUB).reshape(NBLK // unit, unit, 2, CONTRIB // 2).transpose(2, 0, 1, 3)
    order = order.reshape(2, NBLK // unit, -1)
    cos, sin = phase_pair(np.arange(FAC), order.reshape(-1), FAC)
    parts = np.stack([part.reshape(FAC, *order.shape) for part in (cos, sin)], 3)
    return as_bf16(parts.transpose(1, 0, 2, 3, 4).reshape(2, FAC, SUB))


def output_table(groups):
    cos, sin = phase_pair(np.arange(groups * CONTRIB), np.arange(FAC), FAC)
    cos = cos.reshape(groups, CONTRIB, FAC)
    sin = sin.reshape(groups, CONTRIB, FAC)
    real = np.stack([cos, -sin], 1).reshape(groups * LANES, FAC)
    imag = np.stack([sin, cos], 1).reshape(groups * LANES, FAC)
    return as_bf16(np.concatenate([real, imag], 1))


def taper():
    sines = np.sin(np.pi * (np.arange(FAC) + 0.5) / FAC)
    return 0.25 + 0.75 * sines * sines


SINE = [(-1.0) ** k * math.pi ** (2 * k) / math.factorial(2 * k + 1) for k in range(7)]


GAUSS = math.log2(math.e) / (TAPER_SCALE * TAPER_SCALE)
MIDDLE = TILE // 2


def swapped(index, bits):
    result = index
    bit = 1
    while bit <= bits:
        if bits & bit:
            result = result + bit * (1 - 2 * ((index // bit) % 2))
        bit *= 2
    return result


def chains(tile_row, chain):
    blocks = tile_row.shape[1]
    across = jnp.broadcast_to(tile_row[...], (blocks, blocks))
    down = across.T
    above = lax.broadcasted_iota(jnp.int32, (blocks, blocks), 0)
    beside = lax.broadcasted_iota(jnp.int32, (blocks, blocks), 1)
    before = jnp.where((across == down) & (above < beside), above + 1, 0)
    latest = jnp.where(down == beside, above + 1, 0)
    for k, table in enumerate((before, latest)):
        while table.shape[0] > 8:
            half = table.shape[0] // 2
            table = jnp.maximum(table[:half], table[half:])
        for turn in (4, 2, 1):
            table = jnp.maximum(table, pltpu.roll(table, turn, 0))
        chain[k : k + 1, :blocks] = table[:1]


def subgrid_kernel(
    grid_count, vis_count, unitary,
    tiles_hbm, coords_hbm, values_hbm, col_hbm, row_hbm, embed_hbm, scale_hbm, out,
    tile_row, chain, links, coords, values, levels, spread, sums,
    col, table, embed, scale, part, lent, borrowed, spectra, pieces, extra, gathered,
    tile_sem, link_sem, visible_sem, load_sem, share_sem, gather_sem, favour_sem, send1, recv1, recv2,
):
    me_g, me_v = lax.axis_index("grid"), lax.axis_index("vis")
    groups = grid_count // NBLK
    rows_here = out.shape[0]
    half = CONTRIB // 2
    size = grid_count // WAVES
    unit = min(NBLK, size)
    mine = pl.ds(pl.multiple_of(me_v * rows_here, rows_here), rows_here)
    blocks, visible = tile_row.shape[1], coords.shape[0] * LANES // (2 * tile_row.shape[1])
    tall = 2 * visible // LANES
    f32, bf16 = jnp.float32, jnp.bfloat16
    steps = blocks // JOINT

    def loads(i):
        part = pl.ds(i * JOINT * tall, JOINT * tall)
        return (
            pltpu.make_async_copy(coords_hbm.at[part], coords.at[part], visible_sem.at[i, 0]),
            pltpu.make_async_copy(values_hbm.at[part], values.at[part], visible_sem.at[i, 1]),
        )

    for load in loads(0):
        load.start()
    tile_load = pltpu.make_async_copy(tiles_hbm, tile_row, tile_sem)
    tile_load.start()
    for i in range(1, steps):
        for load in loads(i):
            load.start()
    pairs = vis_count // 2
    core, side = me_v % 2, me_v // 2
    mate = (me_g, swapped(me_v, 1))
    chips = grid_count * pairs
    here = me_g * pairs + side
    peers = []
    for k in range(chips - 1):
        chip = k + (k - here + chips) // chips
        peers.append((chip // pairs, chip % pairs * 2 + core))
    barrier = pltpu.get_barrier_semaphore()
    greeted = peers + [mate]
    for peer in greeted:
        pl.semaphore_signal(barrier, inc=1, device_id=peer, device_id_type=MESH)

    @pl.when(here == 0)
    def _():
        for chip in range(1, chips):
            crossed = (chip // pairs, chip % pairs * 2 + 1 - core)
            pl.semaphore_signal(barrier, inc=1, device_id=crossed, device_id_type=MESH)

    @pl.when(here != 0)
    def _():
        pl.semaphore_signal(barrier, inc=1, device_id=(0, 1 - core), device_id_type=MESH)

    tables = [
        pltpu.make_async_copy(col_hbm, col, load_sem.at[0]),
        pltpu.make_async_copy(row_hbm, table, load_sem.at[1]),
        pltpu.make_async_copy(embed_hbm.at[core, mine], embed.at[0], load_sem.at[2]),
        pltpu.make_async_copy(embed_hbm.at[1 - core, mine], embed.at[1], load_sem.at[3]),
        pltpu.make_async_copy(scale_hbm.at[mine], scale, load_sem.at[4]),
    ]
    for load in tables:
        load.start()
    sums[0] = jnp.zeros((TILE, 2 * TILE), f32)
    tile_load.wait()
    chains(tile_row, chain)
    link_load = pltpu.make_async_copy(chain, links, link_sem)
    link_load.start()
    row = lax.broadcasted_iota(jnp.int32, (16, 1), 0).astype(f32)
    lean = (row[:8] - MIDDLE) * (2.0 * GAUSS)
    width = visible // SPLIT
    spots = [
        jnp.broadcast_to((row + 16.0 * a).astype(bf16), (16, width)) for a in range(TILE // 16)
    ]
    even = lax.broadcasted_iota(jnp.int32, (JOINT * tall, LANES), 0) % 2 == 0

    def prepare(b):
        part = pl.ds(b * JOINT * tall, JOINT * tall)
        where = coords[part]
        nearest = jnp.floor(where + 0.5)
        offset = where - nearest
        offset = jnp.where(jnp.abs(offset) < 1e-10, 1e-10, offset)
        square = offset * offset
        wave = square * SINE[5] + SINE[4]
        for k in range(3, -1, -1):
            wave = wave * square + SINE[k]
        half = nearest * 0.5
        odd = (half - jnp.floor(half)) * 4.0 - 1.0
        centred = where - MIDDLE
        wave = (wave * offset) * (odd * jnp.exp2(centred * centred * -GAUSS))
        rows = JOINT * tall
        wave = wave * jnp.where(even, pltpu.roll(wave, rows - 1, 0), pltpu.roll(wave, 1, 0))
        spread[0] = centred
        spread[1] = nearest
        spread[2] = offset
        growth = jnp.exp2(centred * (16.0 * GAUSS))
        spread[3] = growth
        growth = growth * growth
        spread[4] = growth
        levels[...] = values[part] * wave

    def spread_out(ref, i, count):
        rows = [
            jnp.broadcast_to(ref[i + 2 * t : i + 2 * t + 1], (count, LANES))
            for t in range(width // LANES)
        ]
        return jnp.concatenate(rows, 1)

    def wide(ref, i):
        return spread_out(ref, i, 16).astype(bf16)

    def rows(i, paired):
        near = wide(spread.at[1], i)
        apart = wide(spread.at[2], i)
        low = jnp.exp2(spread_out(spread.at[0], i, 8) * lean)
        high = low * spread_out(spread.at[3], i, 8)
        rise = jnp.concatenate([low, high], 0).astype(bf16)
        growth = wide(spread.at[4], i)
        result = []
        if not paired:
            for a in range(TILE // 16):
                result.append(rise * pl.reciprocal((spots[a] - near) - apart, approx=True))
                rise = rise * growth
            return result
        twice = growth * growth
        for a in range(0, TILE // 16, 2):
            here = (spots[a] - near) - apart
            next = (spots[a + 1] - near) - apart
            ratio = rise * pl.reciprocal(here * next, approx=True)
            result += [ratio * next, (ratio * growth) * here]
            rise = rise * twice
        return result

    def piece(i):
        down = rows(i + 1, False)
        right = []
        for c in range(2):
            level = wide(levels, i + c)
            right += [d * level for d in down]
        right = jnp.concatenate(right, 0)
        along = jnp.concatenate(rows(i, False), 0)
        return lax.dot_general(
            along, right, (((1,), (1,)), ((), ())), preferred_element_type=f32
        )

    def several(b, carry):
        for load in loads(b):
            load.wait()
        prepare(b)

        @pl.when(b == 0)
        def _():
            link_load.wait()

        for i in range(JOINT):
            k = b * JOINT + i
            patch = sums[links[0, k]]
            for h in range(SPLIT):
                patch = patch + piece(i * tall + h * (tall // SPLIT))
            sums[k + 1] = patch
        return carry

    lax.fori_loop(0, steps, several, 0)

    down = lax.broadcasted_iota(jnp.int32, (TILE, 2 * TILE), 0) - MIDDLE
    along = lax.broadcasted_iota(jnp.int32, (TILE, 2 * TILE), 1) % TILE - MIDDLE
    power = (down * down + along * along).astype(jnp.float32)
    flip = 1.0 - 2.0 * ((down + along + 2 * TILE) % 2).astype(jnp.float32)
    fall = flip * jnp.exp2(power * -GAUSS)
    for a in range(SUB // TILE):
        for e in range(SUB // TILE):
            spot = (slice(a * TILE, (a + 1) * TILE), slice(e * 2 * TILE, (e + 1) * 2 * TILE))
            part[spot] = (sums[links[1, a * (SUB // TILE) + e]] * fall).astype(bf16)
    for load in tables[:2]:
        load.wait()
    both = []
    for g in range(groups):
        image = jnp.dot(
            part[...], col[:, 2 * LANES * g : 2 * LANES * (g + 1)], preferred_element_type=f32
        )
        image = (image * unitary).astype(bf16)
        both.append(jnp.concatenate([image[:, :LANES], image[:, LANES:]], 0))

    def transformed(which, target):
        rows = table[pl.ds(pl.multiple_of(which * (SUB // 2), SUB // 2), SUB // 2)]
        for g in range(groups):
            result = jnp.dot(rows, both[g], preferred_element_type=f32)
            result = (result * unitary).astype(bf16)
            target[NBLK * g : NBLK * (g + 1)] = result.reshape(NBLK, half, LANES)

    share = pltpu.make_async_remote_copy(
        src_ref=lent, dst_ref=borrowed, send_sem=share_sem.at[0], recv_sem=share_sem.at[1],
        device_id=mate, device_id_type=MESH,
    )

    def scatter(peer):
        return pltpu.make_async_remote_copy(
            src_ref=spectra.at[peer[0]], dst_ref=pieces.at[me_g * pairs + side],
            send_sem=send1, recv_sem=recv1.at[me_g // size], device_id=peer, device_id_type=MESH,
        )

    def gather(w):
        return pltpu.make_async_remote_copy(
            src_ref=gathered.at[w, 0], dst_ref=gathered.at[w, 1], send_sem=gather_sem.at[w, 0],
            recv_sem=gather_sem.at[w, 1], device_id=mate, device_id_type=MESH,
        )

    transformed(1 - core, lent)
    @pl.when(here == 0)
    def _():
        pl.semaphore_wait(barrier, len(greeted) + chips - 1)

    @pl.when(here != 0)
    def _():
        pl.semaphore_wait(barrier, len(greeted) + 1)

    share.start()
    transformed(core, spectra)
    share.wait_recv()
    spectra[...] = (spectra[...].astype(f32) + borrowed[...].astype(f32)).astype(bf16)
    favour = pltpu.make_async_remote_copy(
        src_ref=spectra.at[0], dst_ref=extra.at[here], send_sem=favour_sem,
        recv_sem=recv2.at[me_g // size], device_id=(0, 1 - core), device_id_type=MESH,
    )
    scatter(peers[0]).start()
    favour.start()
    for peer in peers[1:]:
        scatter(peer).start()
    own = pltpu.make_async_copy(
        spectra.at[me_g], pieces.at[me_g * pairs + side], recv1.at[me_g // size]
    )
    own.start()
    for load in tables[2:]:
        load.wait()
    sign = jnp.where(lax.broadcasted_iota(jnp.int32, (1, LANES), 1) < CONTRIB, -1.0, 1.0)
    mixture = [None] * groups

    def mixed(w, h):
        for k in range(size // unit):
            first = w * size + k * unit
            straight = gathered[w, h, k * unit : (k + 1) * unit].reshape(unit * half, LANES)
            turned = pltpu.roll(straight.astype(f32), CONTRIB, 1) * sign
            both = jnp.concatenate([straight, turned.astype(bf16)], 0)
            at = first % NBLK * 2 * half
            result = jnp.dot(
                embed[h, :, at : at + 2 * half * unit], both, preferred_element_type=f32
            )
            g = first // NBLK
            mixture[g] = result if mixture[g] is None else mixture[g] + result

    def summed(ref, sems, w):
        arrived = ref.at[pl.ds(w * size * pairs, size * pairs)]
        pltpu.make_async_copy(arrived, arrived, sems.at[w]).wait()
        whole = arrived[...].reshape(size, pairs, half, LANES).astype(f32)
        return jnp.sum(whole, 1).astype(bf16)

    def finished(w):
        @pl.when(here == 0)
        def _():
            gathered[w, 1] = summed(extra, recv2, w)

        @pl.when(here != 0)
        def _():
            gather(w).wait_recv()

        mixed(w, 1)

    for w in range(WAVES):
        gathered[w, 0] = summed(pieces, recv1, w)

        @pl.when(here != 0)
        def _():
            gather(w).start()

        mixed(w, 0)
        if w > 0:
            finished(w - 1)
    finished(WAVES - 1)
    for g in range(groups):
        out[:, LANES * g : LANES * (g + 1)] = (mixture[g] * scale[...]).astype(bf16)
    share.wait_send()
    others = pieces.at[pl.ds(0, len(peers))]
    pltpu.make_async_copy(others, others, send1).wait()
    favour.wait_send()

    @pl.when(here != 0)
    def _():
        for w in range(WAVES):
            gather(w).wait_send()


def image_kernel(mixture, table, weight, out, image, save_sem):
    rows_here = mixture.shape[0]
    saves = []
    for c in range(2):
        for h in range(SAVES):
            part = slice(h * (rows_here // SAVES), (h + 1) * (rows_here // SAVES))
            result = jnp.dot(
                mixture[part], table[:, c * FAC : (c + 1) * FAC], preferred_element_type=jnp.float32
            )
            image[c, part] = result * weight[...]
            saves.append(
                pltpu.make_async_copy(
                    image.at[c, part], out.at[0, c, part], save_sem.at[c * SAVES + h]
                )
            )
            saves[-1].start()
    for save in saves:
        save.wait()


def shards(grid_count, vis_count, vis_coords, vis_values, tile_index):
    groups = grid_count // NBLK
    half = CONTRIB // 2
    rows_here = FAC // vis_count
    unitary = 1.0 / math.sqrt(SUB)
    bf16, f32 = jnp.bfloat16, jnp.float32
    far = pl.BlockSpec(memory_space=pltpu.HBM)
    inside = pl.BlockSpec(memory_space=pltpu.VMEM)
    dma = pltpu.SemaphoreType.DMA
    blocks = vis_coords.shape[1]
    visible = vis_coords.shape[3]
    tall = 2 * visible // LANES

    def tiled(array):
        array = array.reshape(blocks, 2, visible // LANES, LANES)
        return array.transpose(0, 2, 1, 3).reshape(blocks * tall, LANES)

    row_scale = taper() * (unitary / math.sqrt(CONTRIB * groups))
    row_scale = np.broadcast_to(row_scale[:, None], (FAC, LANES)).astype(np.float32)
    mixture = pl.pallas_call(
        functools.partial(subgrid_kernel, grid_count, vis_count, unitary),
        out_shape=jax.ShapeDtypeStruct((rows_here, groups * LANES), bf16),
        in_specs=[far] * 7,
        out_specs=inside,
        scratch_shapes=[
            pltpu.VMEM((1, blocks), jnp.int32),
            pltpu.VMEM((2, LANES), jnp.int32),
            pltpu.SMEM((2, LANES), jnp.int32),
            pltpu.VMEM((blocks * tall, LANES), f32),
            pltpu.VMEM((blocks * tall, LANES), f32),
            pltpu.VMEM((JOINT * tall, LANES), f32),
            pltpu.VMEM((5, JOINT * tall, LANES), f32),
            pltpu.VMEM((blocks + 1, TILE, 2 * TILE), f32),
            pltpu.VMEM((2 * SUB, 2 * LANES * groups), bf16),
            pltpu.VMEM((SUB, 2 * SUB), bf16),
            pltpu.VMEM((2, rows_here, SUB), bf16),
            pltpu.VMEM((rows_here, LANES), f32),
            pltpu.VMEM((SUB, 2 * SUB), bf16),
            pltpu.VMEM((grid_count, half, LANES), bf16),
            pltpu.VMEM((grid_count, half, LANES), bf16),
            pltpu.VMEM((grid_count, half, LANES), bf16),
            pltpu.VMEM((grid_count * vis_count // 2, half, LANES), bf16),
            pltpu.VMEM((grid_count * vis_count // 2, half, LANES), bf16),
            pltpu.VMEM((WAVES, 2, grid_count // WAVES, half, LANES), bf16),
            dma,
            dma,
            dma((blocks // JOINT, 2)),
            dma((5,)),
            dma((2,)),
            dma((WAVES, 2)),
            dma,
            dma,
            dma((WAVES,)),
            dma((WAVES,)),
        ],
        compiler_params=pltpu.CompilerParams(
            collective_id=0, has_side_effects=True, vmem_limit_bytes=ROOM
        ),
        cost_estimate=pl.CostEstimate(flops=10**10, bytes_accessed=10**6, transcendentals=10**6),
        name="subgrids",
    )(
        *[
            pltpu.with_memory_space_constraint(array, pltpu.HBM)
            for array in (
                tile_index,
                tiled(vis_coords),
                tiled(vis_values),
                jnp.asarray(column_table(groups)),
                jnp.asarray(row_table()),
                jnp.asarray(embed_table(min(NBLK, grid_count // WAVES))),
                jnp.asarray(row_scale),
            )
        ]
    )

    return pl.pallas_call(
        image_kernel,
        out_shape=jax.ShapeDtypeStruct((1, 2, rows_here, FAC), f32),
        in_specs=[inside] * 3,
        out_specs=far,
        scratch_shapes=[pltpu.VMEM((2, rows_here, FAC), f32), dma((2 * SAVES,))],
        compiler_params=pltpu.CompilerParams(vmem_limit_bytes=ROOM),
        name="images",
    )(
        mixture,
        jnp.asarray(output_table(groups)),
        jnp.asarray(taper()[None, :].astype(np.float32)),
    )


def solution(mesh):
    placed = (P("grid", "vis", None, None), P("grid", "vis", None, None), P("grid", "vis"))
    body = functools.partial(shards, mesh.shape["grid"], mesh.shape["vis"])
    return jax.shard_map(
        body, mesh=mesh, in_specs=placed, out_specs=P("grid", None, "vis", None), check_vma=False
    )
```

```python
import functools
import math

import jax
import jax.numpy as jnp
import ml_dtypes
import numpy as np
from jax import lax
from jax.experimental import pallas as pl
from jax.experimental.pallas import tpu as pltpu
from jax.sharding import PartitionSpec as P

SUB = 512
FAC = 1024
CONTRIB = 64
TILE = 64
NBLK = 8
LANES = 2 * CONTRIB
TAPER_SCALE = 16.0
SAVES = 4
WAVES = 1
JOINT = 64
SPLIT = 2
ROOM = 32 * 2**20
MESH = pl.DeviceIdType.MESH


def phase_pair(frequencies, points, length):
    phases = (frequencies[:, None] * points[None, :]) % length
    angles = phases * (2.0 * math.pi / length)
    return np.cos(angles).astype(np.float32), np.sin(angles).astype(np.float32)


def as_bf16(array):
    return array.astype(ml_dtypes.bfloat16)


def column_table(groups):
    cos, sin = phase_pair(np.arange(SUB), np.arange(groups * CONTRIB), SUB)
    across = SUB // TILE
    table = np.zeros((across, 2, TILE, groups, 4, CONTRIB), np.float32)
    cos = cos.reshape(across, TILE, groups, CONTRIB)
    sin = sin.reshape(across, TILE, groups, CONTRIB)
    table[:, 0, :, :, 0], table[:, 1, :, :, 0] = cos, sin
    table[:, 0, :, :, 1], table[:, 1, :, :, 1] = -sin, cos
    table[:, :, :, :, 2] = -table[:, :, :, :, 1]
    table[:, :, :, :, 3] = table[:, :, :, :, 0]
    return as_bf16(table.reshape(2 * SUB, groups * 4 * CONTRIB))


def row_table():
    order = np.arange(SUB).reshape(NBLK, 2, CONTRIB // 2).transpose(1, 0, 2).reshape(SUB)
    cos, sin = phase_pair(order, np.arange(SUB), SUB)
    return as_bf16(np.concatenate([cos, -sin], 1))


def embed_table(unit):
    order = np.arange(SUB).reshape(NBLK // unit, unit, 2, CONTRIB // 2).transpose(2, 0, 1, 3)
    order = order.reshape(2, NBLK // unit, -1)
    cos, sin = phase_pair(np.arange(FAC), order.reshape(-1), FAC)
    parts = np.stack([part.reshape(FAC, *order.shape) for part in (cos, sin)], 3)
    return as_bf16(parts.transpose(1, 0, 2, 3, 4).reshape(2, FAC, SUB))


def output_table(groups):
    cos, sin = phase_pair(np.arange(groups * CONTRIB), np.arange(FAC), FAC)
    cos = cos.reshape(groups, CONTRIB, FAC)
    sin = sin.reshape(groups, CONTRIB, FAC)
    real = np.stack([cos, -sin], 1).reshape(groups * LANES, FAC)
    imag = np.stack([sin, cos], 1).reshape(groups * LANES, FAC)
    return as_bf16(np.concatenate([real, imag], 1))


def taper():
    sines = np.sin(np.pi * (np.arange(FAC) + 0.5) / FAC)
    return 0.25 + 0.75 * sines * sines


SINE = [(-1.0) ** k * math.pi ** (2 * k) / math.factorial(2 * k + 1) for k in range(7)]


GAUSS = math.log2(math.e) / (TAPER_SCALE * TAPER_SCALE)
MIDDLE = TILE // 2


def swapped(index, bits):
    result = index
    bit = 1
    while bit <= bits:
        if bits & bit:
            result = result + bit * (1 - 2 * ((index // bit) % 2))
        bit *= 2
    return result


def chains(tile_row, chain):
    blocks = tile_row.shape[1]
    across = jnp.broadcast_to(tile_row[...], (blocks, blocks))
    down = across.T
    above = lax.broadcasted_iota(jnp.int32, (blocks, blocks), 0)
    beside = lax.broadcasted_iota(jnp.int32, (blocks, blocks), 1)
    before = jnp.where((across == down) & (above < beside), above + 1, 0)
    latest = jnp.where(down == beside, above + 1, 0)
    for k, table in enumerate((before, latest)):
        while table.shape[0] > 8:
            half = table.shape[0] // 2
            table = jnp.maximum(table[:half], table[half:])
        for turn in (4, 2, 1):
            table = jnp.maximum(table, pltpu.roll(table, turn, 0))
        chain[k : k + 1, :blocks] = table[:1]


def subgrid_kernel(
    grid_count, vis_count, unitary,
    tiles_hbm, coords_hbm, values_hbm, col_hbm, row_hbm, embed_hbm, scale_hbm, out,
    tile_row, chain, links, coords, values, levels, spread, sums,
    col, table, embed, scale, part, lent, borrowed, spectra, pieces, extra, gathered,
    tile_sem, link_sem, visible_sem, load_sem, share_sem, gather_sem, favour_sem, send1, recv1, recv2,
):
    me_g, me_v = lax.axis_index("grid"), lax.axis_index("vis")
    groups = grid_count // NBLK
    rows_here = out.shape[0]
    half = CONTRIB // 2
    size = grid_count // WAVES
    unit = min(NBLK, size)
    mine = pl.ds(pl.multiple_of(me_v * rows_here, rows_here), rows_here)
    blocks, visible = tile_row.shape[1], coords.shape[0] * LANES // (2 * tile_row.shape[1])
    tall = 2 * visible // LANES
    f32, bf16 = jnp.float32, jnp.bfloat16
    steps = blocks // JOINT

    def loads(i):
        part = pl.ds(i * JOINT * tall, JOINT * tall)
        return (
            pltpu.make_async_copy(coords_hbm.at[part], coords.at[part], visible_sem.at[i, 0]),
            pltpu.make_async_copy(values_hbm.at[part], values.at[part], visible_sem.at[i, 1]),
        )

    for load in loads(0):
        load.start()
    tile_load = pltpu.make_async_copy(tiles_hbm, tile_row, tile_sem)
    tile_load.start()
    for i in range(1, steps):
        for load in loads(i):
            load.start()
    pairs = vis_count // 2
    core, side = me_v % 2, me_v // 2
    mate = (me_g, swapped(me_v, 1))
    chips = grid_count * pairs
    here = me_g * pairs + side
    peers = []
    for k in range(chips - 1):
        chip = k + (k - here + chips) // chips
        peers.append((chip // pairs, chip % pairs * 2 + core))
    barrier = pltpu.get_barrier_semaphore()
    greeted = peers + [mate]
    for peer in greeted:
        pl.semaphore_signal(barrier, inc=1, device_id=peer, device_id_type=MESH)

    @pl.when(here == 0)
    def _():
        for chip in range(1, chips):
            crossed = (chip // pairs, chip % pairs * 2 + 1 - core)
            pl.semaphore_signal(barrier, inc=1, device_id=crossed, device_id_type=MESH)

    @pl.when(here != 0)
    def _():
        pl.semaphore_signal(barrier, inc=1, device_id=(0, 1 - core), device_id_type=MESH)

    tables = [
        pltpu.make_async_copy(col_hbm, col, load_sem.at[0]),
        pltpu.make_async_copy(row_hbm, table, load_sem.at[1]),
        pltpu.make_async_copy(embed_hbm.at[core, mine], embed.at[0], load_sem.at[2]),
        pltpu.make_async_copy(embed_hbm.at[1 - core, mine], embed.at[1], load_sem.at[3]),
        pltpu.make_async_copy(scale_hbm.at[mine], scale, load_sem.at[4]),
    ]
    for load in tables:
        load.start()
    sums[0] = jnp.zeros((TILE, 2 * TILE), f32)
    tile_load.wait()
    chains(tile_row, chain)
    link_load = pltpu.make_async_copy(chain, links, link_sem)
    link_load.start()
    row = lax.broadcasted_iota(jnp.int32, (16, 1), 0).astype(f32)
    lean = (row[:8] - MIDDLE) * (2.0 * GAUSS)
    width = visible // SPLIT
    spots = [
        jnp.broadcast_to((row + 16.0 * a).astype(bf16), (16, width)) for a in range(TILE // 16)
    ]
    even = lax.broadcasted_iota(jnp.int32, (JOINT * tall, LANES), 0) % 2 == 0

    def prepare(b):
        part = pl.ds(b * JOINT * tall, JOINT * tall)
        where = coords[part]
        nearest = jnp.floor(where + 0.5)
        offset = where - nearest
        offset = jnp.where(jnp.abs(offset) < 1e-10, 1e-10, offset)
        square = offset * offset
        wave = square * SINE[5] + SINE[4]
        for k in range(3, -1, -1):
            wave = wave * square + SINE[k]
        half = nearest * 0.5
        odd = (half - jnp.floor(half)) * 4.0 - 1.0
        centred = where - MIDDLE
        wave = (wave * offset) * (odd * jnp.exp2(centred * centred * -GAUSS))
        rows = JOINT * tall
        wave = wave * jnp.where(even, pltpu.roll(wave, rows - 1, 0), pltpu.roll(wave, 1, 0))
        spread[0] = centred
        spread[1] = nearest
        spread[2] = offset
        growth = jnp.exp2(centred * (16.0 * GAUSS))
        spread[3] = growth
        growth = growth * growth
        spread[4] = growth
        levels[...] = values[part] * wave

    def spread_out(ref, i, count):
        rows = [
            jnp.broadcast_to(ref[i + 2 * t : i + 2 * t + 1], (count, LANES))
            for t in range(width // LANES)
        ]
        return jnp.concatenate(rows, 1)

    def wide(ref, i):
        return spread_out(ref, i, 16).astype(bf16)

    def rows(i, paired):
        near = wide(spread.at[1], i)
        apart = wide(spread.at[2], i)
        low = jnp.exp2(spread_out(spread.at[0], i, 8) * lean)
        high = low * spread_out(spread.at[3], i, 8)
        rise = jnp.concatenate([low, high], 0).astype(bf16)
        growth = wide(spread.at[4], i)
        result = []
        if not paired:
            for a in range(TILE // 16):
                result.append(rise * pl.reciprocal((spots[a] - near) - apart, approx=True))
                rise = rise * growth
            return result
        twice = growth * growth
        for a in range(0, TILE // 16, 2):
            here = (spots[a] - near) - apart
            next = (spots[a + 1] - near) - apart
            ratio = rise * pl.reciprocal(here * next, approx=True)
            result += [ratio * next, (ratio * growth) * here]
            rise = rise * twice
        return result

    def piece(i):
        down = rows(i + 1, False)
        right = []
        for c in range(2):
            level = wide(levels, i + c)
            right += [d * level for d in down]
        right = jnp.concatenate(right, 0)
        along = jnp.concatenate(rows(i, False), 0)
        return lax.dot_general(
            along, right, (((1,), (1,)), ((), ())), preferred_element_type=f32
        )

    def several(b, carry):
        for load in loads(b):
            load.wait()
        prepare(b)

        @pl.when(b == 0)
        def _():
            link_load.wait()

        for i in range(JOINT):
            k = b * JOINT + i
            patch = sums[links[0, k]]
            for h in range(SPLIT):
                patch = patch + piece(i * tall + h * (tall // SPLIT))
            sums[k + 1] = patch
        return carry

    lax.fori_loop(0, steps, several, 0)

    down = lax.broadcasted_iota(jnp.int32, (TILE, 2 * TILE), 0) - MIDDLE
    along = lax.broadcasted_iota(jnp.int32, (TILE, 2 * TILE), 1) % TILE - MIDDLE
    power = (down * down + along * along).astype(jnp.float32)
    flip = 1.0 - 2.0 * ((down + along + 2 * TILE) % 2).astype(jnp.float32)
    fall = flip * jnp.exp2(power * -GAUSS)
    for a in range(SUB // TILE):
        for e in range(SUB // TILE):
            spot = (slice(a * TILE, (a + 1) * TILE), slice(e * 2 * TILE, (e + 1) * 2 * TILE))
            part[spot] = (sums[links[1, a * (SUB // TILE) + e]] * fall).astype(bf16)
    for load in tables[:2]:
        load.wait()
    both = []
    for g in range(groups):
        image = jnp.dot(
            part[...], col[:, 2 * LANES * g : 2 * LANES * (g + 1)], preferred_element_type=f32
        )
        image = (image * unitary).astype(bf16)
        both.append(jnp.concatenate([image[:, :LANES], image[:, LANES:]], 0))

    def transformed(which, target):
        rows = table[pl.ds(pl.multiple_of(which * (SUB // 2), SUB // 2), SUB // 2)]
        for g in range(groups):
            result = jnp.dot(rows, both[g], preferred_element_type=f32)
            result = (result * unitary).astype(bf16)
            target[NBLK * g : NBLK * (g + 1)] = result.reshape(NBLK, half, LANES)

    share = pltpu.make_async_remote_copy(
        src_ref=lent, dst_ref=borrowed, send_sem=share_sem.at[0], recv_sem=share_sem.at[1],
        device_id=mate, device_id_type=MESH,
    )

    def scatter(peer):
        return pltpu.make_async_remote_copy(
            src_ref=spectra.at[peer[0]], dst_ref=pieces.at[me_g * pairs + side],
            send_sem=send1, recv_sem=recv1.at[me_g // size], device_id=peer, device_id_type=MESH,
        )

    def gather(w):
        return pltpu.make_async_remote_copy(
            src_ref=gathered.at[w, 0], dst_ref=gathered.at[w, 1], send_sem=gather_sem.at[w, 0],
            recv_sem=gather_sem.at[w, 1], device_id=mate, device_id_type=MESH,
        )

    transformed(1 - core, lent)
    @pl.when(here == 0)
    def _():
        pl.semaphore_wait(barrier, len(greeted) + chips - 1)

    @pl.when(here != 0)
    def _():
        pl.semaphore_wait(barrier, len(greeted) + 1)

    share.start()
    transformed(core, spectra)
    share.wait_recv()
    spectra[...] = (spectra[...].astype(f32) + borrowed[...].astype(f32)).astype(bf16)
    favour = pltpu.make_async_remote_copy(
        src_ref=spectra.at[0], dst_ref=extra.at[here], send_sem=favour_sem,
        recv_sem=recv2.at[me_g // size], device_id=(0, 1 - core), device_id_type=MESH,
    )
    scatter(peers[0]).start()
    favour.start()
    for peer in peers[1:]:
        scatter(peer).start()
    own = pltpu.make_async_copy(
        spectra.at[me_g], pieces.at[me_g * pairs + side], recv1.at[me_g // size]
    )
    own.start()
    for load in tables[2:]:
        load.wait()
    sign = jnp.where(lax.broadcasted_iota(jnp.int32, (1, LANES), 1) < CONTRIB, -1.0, 1.0)
    mixture = [None] * groups

    def mixed(w, h):
        for k in range(size // unit):
            first = w * size + k * unit
            straight = gathered[w, h, k * unit : (k + 1) * unit].reshape(unit * half, LANES)
            turned = pltpu.roll(straight.astype(f32), CONTRIB, 1) * sign
            both = jnp.concatenate([straight, turned.astype(bf16)], 0)
            at = first % NBLK * 2 * half
            result = jnp.dot(
                embed[h, :, at : at + 2 * half * unit], both, preferred_element_type=f32
            )
            g = first // NBLK
            mixture[g] = result if mixture[g] is None else mixture[g] + result

    def summed(ref, sems, w):
        arrived = ref.at[pl.ds(w * size * pairs, size * pairs)]
        pltpu.make_async_copy(arrived, arrived, sems.at[w]).wait()
        whole = arrived[...].reshape(size, pairs, half, LANES).astype(f32)
        return jnp.sum(whole, 1).astype(bf16)

    def finished(w):
        @pl.when(here == 0)
        def _():
            gathered[w, 1] = summed(extra, recv2, w)

        @pl.when(here != 0)
        def _():
            gather(w).wait_recv()

        mixed(w, 1)

    for w in range(WAVES):
        gathered[w, 0] = summed(pieces, recv1, w)

        @pl.when(here != 0)
        def _():
            gather(w).start()

        mixed(w, 0)
        if w > 0:
            finished(w - 1)
    finished(WAVES - 1)
    for g in range(groups):
        out[:, LANES * g : LANES * (g + 1)] = (mixture[g] * scale[...]).astype(bf16)
    share.wait_send()
    others = pieces.at[pl.ds(0, len(peers))]
    pltpu.make_async_copy(others, others, send1).wait()
    favour.wait_send()

    @pl.when(here != 0)
    def _():
        for w in range(WAVES):
            gather(w).wait_send()


def image_kernel(mixture, table, weight, out, image, save_sem):
    rows_here = mixture.shape[0]
    saves = []
    for c in range(2):
        for h in range(SAVES):
            part = slice(h * (rows_here // SAVES), (h + 1) * (rows_here // SAVES))
            result = jnp.dot(
                mixture[part], table[:, c * FAC : (c + 1) * FAC], preferred_element_type=jnp.float32
            )
            image[c, part] = result * weight[...]
            saves.append(
                pltpu.make_async_copy(
                    image.at[c, part], out.at[0, c, part], save_sem.at[c * SAVES + h]
                )
            )
            saves[-1].start()
    for save in saves:
        save.wait()


def shards(grid_count, vis_count, vis_coords, vis_values, tile_index):
    groups = grid_count // NBLK
    half = CONTRIB // 2
    rows_here = FAC // vis_count
    unitary = 1.0 / math.sqrt(SUB)
    bf16, f32 = jnp.bfloat16, jnp.float32
    far = pl.BlockSpec(memory_space=pltpu.HBM)
    inside = pl.BlockSpec(memory_space=pltpu.VMEM)
    dma = pltpu.SemaphoreType.DMA
    blocks = vis_coords.shape[1]
    visible = vis_coords.shape[3]
    tall = 2 * visible // LANES

    def tiled(array):
        array = array.reshape(blocks, 2, visible // LANES, LANES)
        return array.transpose(0, 2, 1, 3).reshape(blocks * tall, LANES)

    row_scale = taper() * (unitary / math.sqrt(CONTRIB * groups))
    row_scale = np.broadcast_to(row_scale[:, None], (FAC, LANES)).astype(np.float32)
    mixture = pl.pallas_call(
        functools.partial(subgrid_kernel, grid_count, vis_count, unitary),
        out_shape=jax.ShapeDtypeStruct((rows_here, groups * LANES), bf16),
        in_specs=[far] * 7,
        out_specs=inside,
        scratch_shapes=[
            pltpu.VMEM((1, blocks), jnp.int32),
            pltpu.VMEM((2, LANES), jnp.int32),
            pltpu.SMEM((2, LANES), jnp.int32),
            pltpu.VMEM((blocks * tall, LANES), f32),
            pltpu.VMEM((blocks * tall, LANES), f32),
            pltpu.VMEM((JOINT * tall, LANES), f32),
            pltpu.VMEM((5, JOINT * tall, LANES), f32),
            pltpu.VMEM((blocks + 1, TILE, 2 * TILE), f32),
            pltpu.VMEM((2 * SUB, 2 * LANES * groups), bf16),
            pltpu.VMEM((SUB, 2 * SUB), bf16),
            pltpu.VMEM((2, rows_here, SUB), bf16),
            pltpu.VMEM((rows_here, LANES), f32),
            pltpu.VMEM((SUB, 2 * SUB), bf16),
            pltpu.VMEM((grid_count, half, LANES), bf16),
            pltpu.VMEM((grid_count, half, LANES), bf16),
            pltpu.VMEM((grid_count, half, LANES), bf16),
            pltpu.VMEM((grid_count * vis_count // 2, half, LANES), bf16),
            pltpu.VMEM((grid_count * vis_count // 2, half, LANES), bf16),
            pltpu.VMEM((WAVES, 2, grid_count // WAVES, half, LANES), bf16),
            dma,
            dma,
            dma((blocks // JOINT, 2)),
            dma((5,)),
            dma((2,)),
            dma((WAVES, 2)),
            dma,
            dma,
            dma((WAVES,)),
            dma((WAVES,)),
        ],
        compiler_params=pltpu.CompilerParams(
            collective_id=0, has_side_effects=True, vmem_limit_bytes=ROOM
        ),
        cost_estimate=pl.CostEstimate(flops=10**10, bytes_accessed=10**6, transcendentals=10**6),
        name="subgrids",
    )(
        *[
            pltpu.with_memory_space_constraint(array, pltpu.HBM)
            for array in (
                tile_index,
                tiled(vis_coords),
                tiled(vis_values),
                jnp.asarray(column_table(groups)),
                jnp.asarray(row_table()),
                jnp.asarray(embed_table(min(NBLK, grid_count // WAVES))),
                jnp.asarray(row_scale),
            )
        ]
    )

    return pl.pallas_call(
        image_kernel,
        out_shape=jax.ShapeDtypeStruct((1, 2, rows_here, FAC), f32),
        in_specs=[inside] * 3,
        out_specs=far,
        scratch_shapes=[pltpu.VMEM((2, rows_here, FAC), f32), dma((2 * SAVES,))],
        compiler_params=pltpu.CompilerParams(vmem_limit_bytes=ROOM),
        name="images",
    )(
        mixture,
        jnp.asarray(output_table(groups)),
        jnp.asarray(taper()[None, :].astype(np.float32)),
    )


def solution(mesh):
    placed = (P("grid", "vis", None, None), P("grid", "vis", None, None), P("grid", "vis"))
    body = functools.partial(shards, mesh.shape["grid"], mesh.shape["vis"])
    return jax.shard_map(
        body, mesh=mesh, in_specs=placed, out_specs=P("grid", None, "vis", None), check_vma=False
    )
```

```python
import functools
import math

import jax
import jax.numpy as jnp
import ml_dtypes
import numpy as np
from jax import lax
from jax.experimental import pallas as pl
from jax.experimental.pallas import tpu as pltpu
from jax.sharding import PartitionSpec as P

SUB = 512
FAC = 1024
CONTRIB = 64
TILE = 64
NBLK = 8
LANES = 2 * CONTRIB
TAPER_SCALE = 16.0
SAVES = 4
WAVES = 1
JOINT = 64
SPLIT = 2
ROOM = 32 * 2**20
MESH = pl.DeviceIdType.MESH


def phase_pair(frequencies, points, length):
    phases = (frequencies[:, None] * points[None, :]) % length
    angles = phases * (2.0 * math.pi / length)
    return np.cos(angles).astype(np.float32), np.sin(angles).astype(np.float32)


def as_bf16(array):
    return array.astype(ml_dtypes.bfloat16)


def column_table(groups):
    cos, sin = phase_pair(np.arange(SUB), np.arange(groups * CONTRIB), SUB)
    across = SUB // TILE
    table = np.zeros((across, 2, TILE, groups, 4, CONTRIB), np.float32)
    cos = cos.reshape(across, TILE, groups, CONTRIB)
    sin = sin.reshape(across, TILE, groups, CONTRIB)
    table[:, 0, :, :, 0], table[:, 1, :, :, 0] = cos, sin
    table[:, 0, :, :, 1], table[:, 1, :, :, 1] = -sin, cos
    table[:, :, :, :, 2] = -table[:, :, :, :, 1]
    table[:, :, :, :, 3] = table[:, :, :, :, 0]
    return as_bf16(table.reshape(2 * SUB, groups * 4 * CONTRIB))


def row_table():
    order = np.arange(SUB).reshape(NBLK, 2, CONTRIB // 2).transpose(1, 0, 2).reshape(SUB)
    cos, sin = phase_pair(order, np.arange(SUB), SUB)
    return as_bf16(np.concatenate([cos, -sin], 1))


def embed_table(unit):
    order = np.arange(SUB).reshape(NBLK // unit, unit, 2, CONTRIB // 2).transpose(2, 0, 1, 3)
    order = order.reshape(2, NBLK // unit, -1)
    cos, sin = phase_pair(np.arange(FAC), order.reshape(-1), FAC)
    parts = np.stack([part.reshape(FAC, *order.shape) for part in (cos, sin)], 3)
    return as_bf16(parts.transpose(1, 0, 2, 3, 4).reshape(2, FAC, SUB))


def output_table(groups):
    cos, sin = phase_pair(np.arange(groups * CONTRIB), np.arange(FAC), FAC)
    cos = cos.reshape(groups, CONTRIB, FAC)
    sin = sin.reshape(groups, CONTRIB, FAC)
    real = np.stack([cos, -sin], 1).reshape(groups * LANES, FAC)
    imag = np.stack([sin, cos], 1).reshape(groups * LANES, FAC)
    return as_bf16(np.concatenate([real, imag], 1))


def taper():
    sines = np.sin(np.pi * (np.arange(FAC) + 0.5) / FAC)
    return 0.25 + 0.75 * sines * sines


SINE = [(-1.0) ** k * math.pi ** (2 * k) / math.factorial(2 * k + 1) for k in range(7)]


GAUSS = math.log2(math.e) / (TAPER_SCALE * TAPER_SCALE)
MIDDLE = TILE // 2


def swapped(index, bits):
    result = index
    bit = 1
    while bit <= bits:
        if bits & bit:
            result = result + bit * (1 - 2 * ((index // bit) % 2))
        bit *= 2
    return result


def chains(tile_row, chain):
    blocks = tile_row.shape[1]
    across = jnp.broadcast_to(tile_row[...], (blocks, blocks))
    down = across.T
    above = lax.broadcasted_iota(jnp.int32, (blocks, blocks), 0)
    beside = lax.broadcasted_iota(jnp.int32, (blocks, blocks), 1)
    before = jnp.where((across == down) & (above < beside), above + 1, 0)
    latest = jnp.where(down == beside, above + 1, 0)
    for k, table in enumerate((before, latest)):
        while table.shape[0] > 8:
            half = table.shape[0] // 2
            table = jnp.maximum(table[:half], table[half:])
        for turn in (4, 2, 1):
            table = jnp.maximum(table, pltpu.roll(table, turn, 0))
        chain[k : k + 1, :blocks] = table[:1]


def subgrid_kernel(
    grid_count, vis_count, unitary,
    tiles_hbm, coords_hbm, values_hbm, col_hbm, row_hbm, embed_hbm, scale_hbm, out,
    tile_row, chain, links, coords, values, levels, spread, sums,
    col, table, embed, scale, part, lent, borrowed, spectra, pieces, extra, gathered,
    tile_sem, link_sem, visible_sem, load_sem, share_sem, gather_sem, favour_sem, send1, recv1, recv2,
):
    me_g, me_v = lax.axis_index("grid"), lax.axis_index("vis")
    groups = grid_count // NBLK
    rows_here = out.shape[0]
    half = CONTRIB // 2
    size = grid_count // WAVES
    unit = min(NBLK, size)
    mine = pl.ds(pl.multiple_of(me_v * rows_here, rows_here), rows_here)
    blocks, visible = tile_row.shape[1], coords.shape[0] * LANES // (2 * tile_row.shape[1])
    tall = 2 * visible // LANES
    f32, bf16 = jnp.float32, jnp.bfloat16
    steps = blocks // JOINT

    def loads(i):
        part = pl.ds(i * JOINT * tall, JOINT * tall)
        return (
            pltpu.make_async_copy(coords_hbm.at[part], coords.at[part], visible_sem.at[i, 0]),
            pltpu.make_async_copy(values_hbm.at[part], values.at[part], visible_sem.at[i, 1]),
        )

    for load in loads(0):
        load.start()
    tile_load = pltpu.make_async_copy(tiles_hbm, tile_row, tile_sem)
    tile_load.start()
    for i in range(1, steps):
        for load in loads(i):
            load.start()
    pairs = vis_count // 2
    core, side = me_v % 2, me_v // 2
    mate = (me_g, swapped(me_v, 1))
    chips = grid_count * pairs
    here = me_g * pairs + side
    peers = []
    for k in range(chips - 1):
        chip = k + (k - here + chips) // chips
        peers.append((chip // pairs, chip % pairs * 2 + core))
    barrier = pltpu.get_barrier_semaphore()
    greeted = peers + [mate]
    for peer in greeted:
        pl.semaphore_signal(barrier, inc=1, device_id=peer, device_id_type=MESH)

    @pl.when(here == 0)
    def _():
        for chip in range(1, chips):
            crossed = (chip // pairs, chip % pairs * 2 + 1 - core)
            pl.semaphore_signal(barrier, inc=1, device_id=crossed, device_id_type=MESH)

    @pl.when(here != 0)
    def _():
        pl.semaphore_signal(barrier, inc=1, device_id=(0, 1 - core), device_id_type=MESH)

    tables = [
        pltpu.make_async_copy(col_hbm, col, load_sem.at[0]),
        pltpu.make_async_copy(row_hbm, table, load_sem.at[1]),
        pltpu.make_async_copy(embed_hbm.at[core, mine], embed.at[0], load_sem.at[2]),
        pltpu.make_async_copy(embed_hbm.at[1 - core, mine], embed.at[1], load_sem.at[3]),
        pltpu.make_async_copy(scale_hbm.at[mine], scale, load_sem.at[4]),
    ]
    for load in tables:
        load.start()
    sums[0] = jnp.zeros((TILE, 2 * TILE), f32)
    tile_load.wait()
    chains(tile_row, chain)
    link_load = pltpu.make_async_copy(chain, links, link_sem)
    link_load.start()
    row = lax.broadcasted_iota(jnp.int32, (16, 1), 0).astype(f32)
    lean = (row[:8] - MIDDLE) * (2.0 * GAUSS)
    width = visible // SPLIT
    spots = [
        jnp.broadcast_to((row + 16.0 * a).astype(bf16), (16, width)) for a in range(TILE // 16)
    ]
    even = lax.broadcasted_iota(jnp.int32, (JOINT * tall, LANES), 0) % 2 == 0

    def prepare(b):
        part = pl.ds(b * JOINT * tall, JOINT * tall)
        where = coords[part]
        nearest = jnp.floor(where + 0.5)
        offset = where - nearest
        offset = jnp.where(jnp.abs(offset) < 1e-10, 1e-10, offset)
        square = offset * offset
        wave = square * SINE[5] + SINE[4]
        for k in range(3, -1, -1):
            wave = wave * square + SINE[k]
        half = nearest * 0.5
        odd = (half - jnp.floor(half)) * 4.0 - 1.0
        centred = where - MIDDLE
        wave = (wave * offset) * (odd * jnp.exp2(centred * centred * -GAUSS))
        rows = JOINT * tall
        wave = wave * jnp.where(even, pltpu.roll(wave, rows - 1, 0), pltpu.roll(wave, 1, 0))
        spread[0] = centred
        spread[1] = nearest
        spread[2] = offset
        growth = jnp.exp2(centred * (16.0 * GAUSS))
        spread[3] = growth
        growth = growth * growth
        spread[4] = growth
        levels[...] = values[part] * wave

    def spread_out(ref, i, count):
        rows = [
            jnp.broadcast_to(ref[i + 2 * t : i + 2 * t + 1], (count, LANES))
            for t in range(width // LANES)
        ]
        return jnp.concatenate(rows, 1)

    def wide(ref, i):
        return spread_out(ref, i, 16).astype(bf16)

    def rows(i, paired):
        near = wide(spread.at[1], i)
        apart = wide(spread.at[2], i)
        low = jnp.exp2(spread_out(spread.at[0], i, 8) * lean)
        high = low * spread_out(spread.at[3], i, 8)
        rise = jnp.concatenate([low, high], 0).astype(bf16)
        growth = wide(spread.at[4], i)
        result = []
        if not paired:
            for a in range(TILE // 16):
                result.append(rise * pl.reciprocal((spots[a] - near) - apart, approx=True))
                rise = rise * growth
            return result
        twice = growth * growth
        for a in range(0, TILE // 16, 2):
            here = (spots[a] - near) - apart
            next = (spots[a + 1] - near) - apart
            ratio = rise * pl.reciprocal(here * next, approx=True)
            result += [ratio * next, (ratio * growth) * here]
            rise = rise * twice
        return result

    def piece(i):
        down = rows(i + 1, False)
        right = []
        for c in range(2):
            level = wide(levels, i + c)
            right += [d * level for d in down]
        right = jnp.concatenate(right, 0)
        along = jnp.concatenate(rows(i, False), 0)
        return lax.dot_general(
            along, right, (((1,), (1,)), ((), ())), preferred_element_type=f32
        )

    def several(b, carry):
        for load in loads(b):
            load.wait()
        prepare(b)

        @pl.when(b == 0)
        def _():
            link_load.wait()

        for i in range(JOINT):
            k = b * JOINT + i
            patch = sums[links[0, k]]
            for h in range(SPLIT):
                patch = patch + piece(i * tall + h * (tall // SPLIT))
            sums[k + 1] = patch
        return carry

    lax.fori_loop(0, steps, several, 0)

    down = lax.broadcasted_iota(jnp.int32, (TILE, 2 * TILE), 0) - MIDDLE
    along = lax.broadcasted_iota(jnp.int32, (TILE, 2 * TILE), 1) % TILE - MIDDLE
    power = (down * down + along * along).astype(jnp.float32)
    flip = 1.0 - 2.0 * ((down + along + 2 * TILE) % 2).astype(jnp.float32)
    fall = flip * jnp.exp2(power * -GAUSS)
    for a in range(SUB // TILE):
        for e in range(SUB // TILE):
            spot = (slice(a * TILE, (a + 1) * TILE), slice(e * 2 * TILE, (e + 1) * 2 * TILE))
            part[spot] = (sums[links[1, a * (SUB // TILE) + e]] * fall).astype(bf16)
    for load in tables[:2]:
        load.wait()
    both = []
    for g in range(groups):
        image = jnp.dot(
            part[...], col[:, 2 * LANES * g : 2 * LANES * (g + 1)], preferred_element_type=f32
        )
        image = (image * unitary).astype(bf16)
        both.append(jnp.concatenate([image[:, :LANES], image[:, LANES:]], 0))

    facets = grid_count // 2

    def transformed(which, target, p):
        count = min(NBLK, facets)
        first = which * (SUB // 2) + (p * facets % NBLK) * half
        rows = table[pl.ds(pl.multiple_of(first, half), count * half)]
        for f in range(p * facets, (p + 1) * facets, count):
            result = jnp.dot(rows, both[f // NBLK], preferred_element_type=f32)
            result = (result * unitary).astype(bf16)
            target[f : f + count] = result.reshape(count, half, LANES)

    def share(p):
        part = pl.ds(p * facets, facets)
        return pltpu.make_async_remote_copy(
            src_ref=lent.at[part], dst_ref=borrowed.at[part], send_sem=share_sem.at[0, p],
            recv_sem=share_sem.at[1, p], device_id=mate, device_id_type=MESH,
        )

    def combined(p):
        part = slice(p * facets, (p + 1) * facets)
        transformed(core, spectra, p)
        share(p).wait_recv()
        spectra[part] = (spectra[part].astype(f32) + borrowed[part].astype(f32)).astype(bf16)

    def scatter(peer):
        return pltpu.make_async_remote_copy(
            src_ref=spectra.at[peer[0]], dst_ref=pieces.at[me_g * pairs + side],
            send_sem=send1, recv_sem=recv1.at[me_g // size], device_id=peer, device_id_type=MESH,
        )

    def gather(w):
        return pltpu.make_async_remote_copy(
            src_ref=gathered.at[w, 0], dst_ref=gathered.at[w, 1], send_sem=gather_sem.at[w, 0],
            recv_sem=gather_sem.at[w, 1], device_id=mate, device_id_type=MESH,
        )

    transformed(1 - core, lent, 0)
    @pl.when(here == 0)
    def _():
        pl.semaphore_wait(barrier, len(greeted) + chips - 1)

    @pl.when(here != 0)
    def _():
        pl.semaphore_wait(barrier, len(greeted) + 1)

    share(0).start()
    transformed(1 - core, lent, 1)
    share(1).start()
    combined(0)
    favour = pltpu.make_async_remote_copy(
        src_ref=spectra.at[0], dst_ref=extra.at[here], send_sem=favour_sem,
        recv_sem=recv2.at[me_g // size], device_id=(0, 1 - core), device_id_type=MESH,
    )
    early = chips // 2 - 1
    scatter(peers[0]).start()
    favour.start()
    for peer in peers[1:early]:
        scatter(peer).start()
    combined(1)
    for peer in peers[early:]:
        scatter(peer).start()
    own = pltpu.make_async_copy(
        spectra.at[me_g], pieces.at[me_g * pairs + side], recv1.at[me_g // size]
    )
    own.start()
    for load in tables[2:]:
        load.wait()
    sign = jnp.where(lax.broadcasted_iota(jnp.int32, (1, LANES), 1) < CONTRIB, -1.0, 1.0)
    mixture = [None] * groups

    def mixed(w, h):
        for k in range(size // unit):
            first = w * size + k * unit
            straight = gathered[w, h, k * unit : (k + 1) * unit].reshape(unit * half, LANES)
            turned = pltpu.roll(straight.astype(f32), CONTRIB, 1) * sign
            both = jnp.concatenate([straight, turned.astype(bf16)], 0)
            at = first % NBLK * 2 * half
            result = jnp.dot(
                embed[h, :, at : at + 2 * half * unit], both, preferred_element_type=f32
            )
            g = first // NBLK
            mixture[g] = result if mixture[g] is None else mixture[g] + result

    def summed(ref, sems, w):
        arrived = ref.at[pl.ds(w * size * pairs, size * pairs)]
        pltpu.make_async_copy(arrived, arrived, sems.at[w]).wait()
        whole = arrived[...].reshape(size, pairs, half, LANES).astype(f32)
        return jnp.sum(whole, 1).astype(bf16)

    def finished(w):
        @pl.when(here == 0)
        def _():
            gathered[w, 1] = summed(extra, recv2, w)

        @pl.when(here != 0)
        def _():
            gather(w).wait_recv()

        mixed(w, 1)

    for w in range(WAVES):
        gathered[w, 0] = summed(pieces, recv1, w)

        @pl.when(here != 0)
        def _():
            gather(w).start()

        mixed(w, 0)
        if w > 0:
            finished(w - 1)
    finished(WAVES - 1)
    for g in range(groups):
        out[:, LANES * g : LANES * (g + 1)] = (mixture[g] * scale[...]).astype(bf16)
    for p in range(2):
        share(p).wait_send()
    others = pieces.at[pl.ds(0, len(peers))]
    pltpu.make_async_copy(others, others, send1).wait()
    favour.wait_send()

    @pl.when(here != 0)
    def _():
        for w in range(WAVES):
            gather(w).wait_send()


def image_kernel(mixture, table, weight, out, image, save_sem):
    rows_here = mixture.shape[0]
    saves = []
    for c in range(2):
        for h in range(SAVES):
            part = slice(h * (rows_here // SAVES), (h + 1) * (rows_here // SAVES))
            result = jnp.dot(
                mixture[part], table[:, c * FAC : (c + 1) * FAC], preferred_element_type=jnp.float32
            )
            image[c, part] = result * weight[...]
            saves.append(
                pltpu.make_async_copy(
                    image.at[c, part], out.at[0, c, part], save_sem.at[c * SAVES + h]
                )
            )
            saves[-1].start()
    for save in saves:
        save.wait()


def shards(grid_count, vis_count, vis_coords, vis_values, tile_index):
    groups = grid_count // NBLK
    half = CONTRIB // 2
    rows_here = FAC // vis_count
    unitary = 1.0 / math.sqrt(SUB)
    bf16, f32 = jnp.bfloat16, jnp.float32
    far = pl.BlockSpec(memory_space=pltpu.HBM)
    inside = pl.BlockSpec(memory_space=pltpu.VMEM)
    dma = pltpu.SemaphoreType.DMA
    blocks = vis_coords.shape[1]
    visible = vis_coords.shape[3]
    tall = 2 * visible // LANES

    def tiled(array):
        array = array.reshape(blocks, 2, visible // LANES, LANES)
        return array.transpose(0, 2, 1, 3).reshape(blocks * tall, LANES)

    row_scale = taper() * (unitary / math.sqrt(CONTRIB * groups))
    row_scale = np.broadcast_to(row_scale[:, None], (FAC, LANES)).astype(np.float32)
    mixture = pl.pallas_call(
        functools.partial(subgrid_kernel, grid_count, vis_count, unitary),
        out_shape=jax.ShapeDtypeStruct((rows_here, groups * LANES), bf16),
        in_specs=[far] * 7,
        out_specs=inside,
        scratch_shapes=[
            pltpu.VMEM((1, blocks), jnp.int32),
            pltpu.VMEM((2, LANES), jnp.int32),
            pltpu.SMEM((2, LANES), jnp.int32),
            pltpu.VMEM((blocks * tall, LANES), f32),
            pltpu.VMEM((blocks * tall, LANES), f32),
            pltpu.VMEM((JOINT * tall, LANES), f32),
            pltpu.VMEM((5, JOINT * tall, LANES), f32),
            pltpu.VMEM((blocks + 1, TILE, 2 * TILE), f32),
            pltpu.VMEM((2 * SUB, 2 * LANES * groups), bf16),
            pltpu.VMEM((SUB, 2 * SUB), bf16),
            pltpu.VMEM((2, rows_here, SUB), bf16),
            pltpu.VMEM((rows_here, LANES), f32),
            pltpu.VMEM((SUB, 2 * SUB), bf16),
            pltpu.VMEM((grid_count, half, LANES), bf16),
            pltpu.VMEM((grid_count, half, LANES), bf16),
            pltpu.VMEM((grid_count, half, LANES), bf16),
            pltpu.VMEM((grid_count * vis_count // 2, half, LANES), bf16),
            pltpu.VMEM((grid_count * vis_count // 2, half, LANES), bf16),
            pltpu.VMEM((WAVES, 2, grid_count // WAVES, half, LANES), bf16),
            dma,
            dma,
            dma((blocks // JOINT, 2)),
            dma((5,)),
            dma((2, 2)),
            dma((WAVES, 2)),
            dma,
            dma,
            dma((WAVES,)),
            dma((WAVES,)),
        ],
        compiler_params=pltpu.CompilerParams(
            collective_id=0, has_side_effects=True, vmem_limit_bytes=ROOM
        ),
        cost_estimate=pl.CostEstimate(flops=10**10, bytes_accessed=10**6, transcendentals=10**6),
        name="subgrids",
    )(
        *[
            pltpu.with_memory_space_constraint(array, pltpu.HBM)
            for array in (
                tile_index,
                tiled(vis_coords),
                tiled(vis_values),
                jnp.asarray(column_table(groups)),
                jnp.asarray(row_table()),
                jnp.asarray(embed_table(min(NBLK, grid_count // WAVES))),
                jnp.asarray(row_scale),
            )
        ]
    )

    return pl.pallas_call(
        image_kernel,
        out_shape=jax.ShapeDtypeStruct((1, 2, rows_here, FAC), f32),
        in_specs=[inside] * 3,
        out_specs=far,
        scratch_shapes=[pltpu.VMEM((2, rows_here, FAC), f32), dma((2 * SAVES,))],
        compiler_params=pltpu.CompilerParams(vmem_limit_bytes=ROOM),
        name="images",
    )(
        mixture,
        jnp.asarray(output_table(groups)),
        jnp.asarray(taper()[None, :].astype(np.float32)),
    )


def solution(mesh):
    placed = (P("grid", "vis", None, None), P("grid", "vis", None, None), P("grid", "vis"))
    body = functools.partial(shards, mesh.shape["grid"], mesh.shape["vis"])
    return jax.shard_map(
        body, mesh=mesh, in_specs=placed, out_specs=P("grid", None, "vis", None), check_vma=False
    )
```

```python
import functools
import math

import jax
import jax.numpy as jnp
import ml_dtypes
import numpy as np
from jax import lax
from jax.experimental import pallas as pl
from jax.experimental.pallas import tpu as pltpu
from jax.sharding import PartitionSpec as P

SUB = 512
FAC = 1024
CONTRIB = 64
TILE = 64
NBLK = 8
LANES = 2 * CONTRIB
TAPER_SCALE = 16.0
SAVES = 4
WAVES = 1
JOINT = 64
SPLIT = 2
ROOM = 32 * 2**20
MESH = pl.DeviceIdType.MESH


def phase_pair(frequencies, points, length):
    phases = (frequencies[:, None] * points[None, :]) % length
    angles = phases * (2.0 * math.pi / length)
    return np.cos(angles).astype(np.float32), np.sin(angles).astype(np.float32)


def as_bf16(array):
    return array.astype(ml_dtypes.bfloat16)


def column_table(groups):
    cos, sin = phase_pair(np.arange(SUB), np.arange(groups * CONTRIB), SUB)
    across = SUB // TILE
    table = np.zeros((across, 2, TILE, groups, 4, CONTRIB), np.float32)
    cos = cos.reshape(across, TILE, groups, CONTRIB)
    sin = sin.reshape(across, TILE, groups, CONTRIB)
    table[:, 0, :, :, 0], table[:, 1, :, :, 0] = cos, sin
    table[:, 0, :, :, 1], table[:, 1, :, :, 1] = -sin, cos
    table[:, :, :, :, 2] = -table[:, :, :, :, 1]
    table[:, :, :, :, 3] = table[:, :, :, :, 0]
    return as_bf16(table.reshape(2 * SUB, groups * 4 * CONTRIB))


def row_table():
    order = np.arange(SUB).reshape(NBLK, 2, CONTRIB // 2).transpose(1, 0, 2).reshape(SUB)
    cos, sin = phase_pair(order, np.arange(SUB), SUB)
    return as_bf16(np.concatenate([cos, -sin], 1))


def embed_table(unit):
    order = np.arange(SUB).reshape(NBLK // unit, unit, 2, CONTRIB // 2).transpose(2, 0, 1, 3)
    order = order.reshape(2, NBLK // unit, -1)
    cos, sin = phase_pair(np.arange(FAC), order.reshape(-1), FAC)
    parts = np.stack([part.reshape(FAC, *order.shape) for part in (cos, sin)], 3)
    return as_bf16(parts.transpose(1, 0, 2, 3, 4).reshape(2, FAC, SUB))


def output_table(groups):
    cos, sin = phase_pair(np.arange(groups * CONTRIB), np.arange(FAC), FAC)
    cos = cos.reshape(groups, CONTRIB, FAC)
    sin = sin.reshape(groups, CONTRIB, FAC)
    real = np.stack([cos, -sin], 1).reshape(groups * LANES, FAC)
    imag = np.stack([sin, cos], 1).reshape(groups * LANES, FAC)
    return as_bf16(np.concatenate([real, imag], 1))


def taper():
    sines = np.sin(np.pi * (np.arange(FAC) + 0.5) / FAC)
    return 0.25 + 0.75 * sines * sines


SINE = [(-1.0) ** k * math.pi ** (2 * k) / math.factorial(2 * k + 1) for k in range(7)]


GAUSS = math.log2(math.e) / (TAPER_SCALE * TAPER_SCALE)
MIDDLE = TILE // 2


def swapped(index, bits):
    result = index
    bit = 1
    while bit <= bits:
        if bits & bit:
            result = result + bit * (1 - 2 * ((index // bit) % 2))
        bit *= 2
    return result


def chains(tile_row, chain):
    blocks = tile_row.shape[1]
    across = jnp.broadcast_to(tile_row[...], (blocks, blocks))
    down = across.T
    above = lax.broadcasted_iota(jnp.int32, (blocks, blocks), 0)
    beside = lax.broadcasted_iota(jnp.int32, (blocks, blocks), 1)
    before = jnp.where((across == down) & (above < beside), above + 1, 0)
    latest = jnp.where(down == beside, above + 1, 0)
    for k, table in enumerate((before, latest)):
        while table.shape[0] > 8:
            half = table.shape[0] // 2
            table = jnp.maximum(table[:half], table[half:])
        for turn in (4, 2, 1):
            table = jnp.maximum(table, pltpu.roll(table, turn, 0))
        chain[k : k + 1, :blocks] = table[:1]


def subgrid_kernel(
    grid_count, vis_count, unitary,
    tiles_hbm, coords_hbm, values_hbm, col_hbm, row_hbm, embed_hbm, scale_hbm, out,
    tile_row, chain, links, coords, values, levels, spread, sums,
    col, table, embed, scale, part, lent, borrowed, spectra, pieces, extra, gathered,
    tile_sem, link_sem, visible_sem, load_sem, share_sem, gather_sem, favour_sem, send1, recv1, recv2,
):
    me_g, me_v = lax.axis_index("grid"), lax.axis_index("vis")
    groups = grid_count // NBLK
    rows_here = out.shape[0]
    half = CONTRIB // 2
    size = grid_count // WAVES
    unit = min(NBLK, size)
    mine = pl.ds(pl.multiple_of(me_v * rows_here, rows_here), rows_here)
    blocks, visible = tile_row.shape[1], coords.shape[0] * LANES // (2 * tile_row.shape[1])
    tall = 2 * visible // LANES
    f32, bf16 = jnp.float32, jnp.bfloat16
    steps = blocks // JOINT

    def loads(i):
        part = pl.ds(i * JOINT * tall, JOINT * tall)
        return (
            pltpu.make_async_copy(coords_hbm.at[part], coords.at[part], visible_sem.at[i, 0]),
            pltpu.make_async_copy(values_hbm.at[part], values.at[part], visible_sem.at[i, 1]),
        )

    for load in loads(0):
        load.start()
    tile_load = pltpu.make_async_copy(tiles_hbm, tile_row, tile_sem)
    tile_load.start()
    for i in range(1, steps):
        for load in loads(i):
            load.start()
    pairs = vis_count // 2
    core, side = me_v % 2, me_v // 2
    mate = (me_g, swapped(me_v, 1))
    chips = grid_count * pairs
    here = me_g * pairs + side
    peers = []
    for k in range(chips - 1):
        chip = k + (k - here + chips) // chips
        peers.append((chip // pairs, chip % pairs * 2 + core))
    barrier = pltpu.get_barrier_semaphore()
    greeted = peers + [mate]
    for peer in greeted:
        pl.semaphore_signal(barrier, inc=1, device_id=peer, device_id_type=MESH)

    @pl.when(here == 0)
    def _():
        for chip in range(1, chips):
            crossed = (chip // pairs, chip % pairs * 2 + 1 - core)
            pl.semaphore_signal(barrier, inc=1, device_id=crossed, device_id_type=MESH)

    @pl.when(here != 0)
    def _():
        pl.semaphore_signal(barrier, inc=1, device_id=(0, 1 - core), device_id_type=MESH)

    tables = [
        pltpu.make_async_copy(col_hbm, col, load_sem.at[0]),
        pltpu.make_async_copy(row_hbm, table, load_sem.at[1]),
        pltpu.make_async_copy(embed_hbm.at[core, mine], embed.at[0], load_sem.at[2]),
        pltpu.make_async_copy(embed_hbm.at[1 - core, mine], embed.at[1], load_sem.at[3]),
        pltpu.make_async_copy(scale_hbm.at[mine], scale, load_sem.at[4]),
    ]
    for load in tables:
        load.start()
    sums[0] = jnp.zeros((TILE, 2 * TILE), f32)
    tile_load.wait()
    chains(tile_row, chain)
    link_load = pltpu.make_async_copy(chain, links, link_sem)
    link_load.start()
    row = lax.broadcasted_iota(jnp.int32, (16, 1), 0).astype(f32)
    lean = (row[:8] - MIDDLE) * (2.0 * GAUSS)
    width = visible // SPLIT
    spots = [
        jnp.broadcast_to((row + 16.0 * a).astype(bf16), (16, width)) for a in range(TILE // 16)
    ]
    even = lax.broadcasted_iota(jnp.int32, (JOINT * tall, LANES), 0) % 2 == 0

    def prepare(b):
        part = pl.ds(b * JOINT * tall, JOINT * tall)
        where = coords[part]
        nearest = jnp.floor(where + 0.5)
        offset = where - nearest
        offset = jnp.where(jnp.abs(offset) < 1e-10, 1e-10, offset)
        square = offset * offset
        wave = square * SINE[5] + SINE[4]
        for k in range(3, -1, -1):
            wave = wave * square + SINE[k]
        half = nearest * 0.5
        odd = (half - jnp.floor(half)) * 4.0 - 1.0
        centred = where - MIDDLE
        wave = (wave * offset) * (odd * jnp.exp2(centred * centred * -GAUSS))
        rows = JOINT * tall
        wave = wave * jnp.where(even, pltpu.roll(wave, rows - 1, 0), pltpu.roll(wave, 1, 0))
        spread[0] = centred
        spread[1] = nearest
        spread[2] = offset
        growth = jnp.exp2(centred * (16.0 * GAUSS))
        spread[3] = growth
        growth = growth * growth
        spread[4] = growth
        levels[...] = values[part] * wave

    def spread_out(ref, i, count):
        rows = [
            jnp.broadcast_to(ref[i + 2 * t : i + 2 * t + 1], (count, LANES))
            for t in range(width // LANES)
        ]
        return jnp.concatenate(rows, 1)

    def wide(ref, i):
        return spread_out(ref, i, 16).astype(bf16)

    def rows(i, paired):
        near = wide(spread.at[1], i)
        apart = wide(spread.at[2], i)
        low = jnp.exp2(spread_out(spread.at[0], i, 8) * lean)
        high = low * spread_out(spread.at[3], i, 8)
        rise = jnp.concatenate([low, high], 0).astype(bf16)
        growth = wide(spread.at[4], i)
        result = []
        if not paired:
            for a in range(TILE // 16):
                result.append(rise * pl.reciprocal((spots[a] - near) - apart, approx=True))
                rise = rise * growth
            return result
        twice = growth * growth
        for a in range(0, TILE // 16, 2):
            here = (spots[a] - near) - apart
            next = (spots[a + 1] - near) - apart
            ratio = rise * pl.reciprocal(here * next, approx=True)
            result += [ratio * next, (ratio * growth) * here]
            rise = rise * twice
        return result

    def piece(i):
        along = jnp.concatenate(rows(i, False), 0)
        down = rows(i + 1, False)
        right = []
        for c in range(2):
            level = wide(levels, i + c)
            right += [d * level for d in down]
        right = jnp.concatenate(right, 0)
        return lax.dot_general(
            along, right, (((1,), (1,)), ((), ())), preferred_element_type=f32
        )

    def several(b, carry):
        for load in loads(b):
            load.wait()
        prepare(b)

        @pl.when(b == 0)
        def _():
            link_load.wait()

        for i in range(JOINT):
            k = b * JOINT + i
            patch = sums[links[0, k]]
            for h in range(SPLIT):
                patch = patch + piece(i * tall + h * (tall // SPLIT))
            sums[k + 1] = patch
        return carry

    lax.fori_loop(0, steps, several, 0)

    down = lax.broadcasted_iota(jnp.int32, (TILE, 2 * TILE), 0) - MIDDLE
    along = lax.broadcasted_iota(jnp.int32, (TILE, 2 * TILE), 1) % TILE - MIDDLE
    power = (down * down + along * along).astype(jnp.float32)
    flip = 1.0 - 2.0 * ((down + along + 2 * TILE) % 2).astype(jnp.float32)
    fall = flip * jnp.exp2(power * -GAUSS)
    for a in range(SUB // TILE):
        for e in range(SUB // TILE):
            spot = (slice(a * TILE, (a + 1) * TILE), slice(e * 2 * TILE, (e + 1) * 2 * TILE))
            part[spot] = (sums[links[1, a * (SUB // TILE) + e]] * fall).astype(bf16)
    for load in tables[:2]:
        load.wait()
    both = []
    for g in range(groups):
        image = jnp.dot(
            part[...], col[:, 2 * LANES * g : 2 * LANES * (g + 1)], preferred_element_type=f32
        )
        image = (image * unitary).astype(bf16)
        both.append(jnp.concatenate([image[:, :LANES], image[:, LANES:]], 0))

    facets = grid_count // 2

    def transformed(which, target, p):
        count = min(NBLK, facets)
        first = which * (SUB // 2) + (p * facets % NBLK) * half
        rows = table[pl.ds(pl.multiple_of(first, half), count * half)]
        for f in range(p * facets, (p + 1) * facets, count):
            result = jnp.dot(rows, both[f // NBLK], preferred_element_type=f32)
            result = (result * unitary).astype(bf16)
            target[f : f + count] = result.reshape(count, half, LANES)

    def share(p):
        part = pl.ds(p * facets, facets)
        return pltpu.make_async_remote_copy(
            src_ref=lent.at[part], dst_ref=borrowed.at[part], send_sem=share_sem.at[0, p],
            recv_sem=share_sem.at[1, p], device_id=mate, device_id_type=MESH,
        )

    def combined(p):
        part = slice(p * facets, (p + 1) * facets)
        transformed(core, spectra, p)
        share(p).wait_recv()
        spectra[part] = (spectra[part].astype(f32) + borrowed[part].astype(f32)).astype(bf16)

    def scatter(peer):
        return pltpu.make_async_remote_copy(
            src_ref=spectra.at[peer[0]], dst_ref=pieces.at[me_g * pairs + side],
            send_sem=send1, recv_sem=recv1.at[me_g // size], device_id=peer, device_id_type=MESH,
        )

    def gather(w):
        return pltpu.make_async_remote_copy(
            src_ref=gathered.at[w, 0], dst_ref=gathered.at[w, 1], send_sem=gather_sem.at[w, 0],
            recv_sem=gather_sem.at[w, 1], device_id=mate, device_id_type=MESH,
        )

    transformed(1 - core, lent, 0)
    @pl.when(here == 0)
    def _():
        pl.semaphore_wait(barrier, len(greeted) + chips - 1)

    @pl.when(here != 0)
    def _():
        pl.semaphore_wait(barrier, len(greeted) + 1)

    share(0).start()
    transformed(1 - core, lent, 1)
    share(1).start()
    combined(0)
    favour = pltpu.make_async_remote_copy(
        src_ref=spectra.at[0], dst_ref=extra.at[here], send_sem=favour_sem,
        recv_sem=recv2.at[me_g // size], device_id=(0, 1 - core), device_id_type=MESH,
    )
    early = chips // 2 - 1
    scatter(peers[0]).start()
    favour.start()
    for peer in peers[1:early]:
        scatter(peer).start()
    combined(1)
    for peer in peers[early:]:
        scatter(peer).start()
    own = pltpu.make_async_copy(
        spectra.at[me_g], pieces.at[me_g * pairs + side], recv1.at[me_g // size]
    )
    own.start()
    for load in tables[2:]:
        load.wait()
    sign = jnp.where(lax.broadcasted_iota(jnp.int32, (1, LANES), 1) < CONTRIB, -1.0, 1.0)
    mixture = [None] * groups

    def mixed(w, h):
        for k in range(size // unit):
            first = w * size + k * unit
            straight = gathered[w, h, k * unit : (k + 1) * unit].reshape(unit * half, LANES)
            turned = pltpu.roll(straight.astype(f32), CONTRIB, 1) * sign
            both = jnp.concatenate([straight, turned.astype(bf16)], 0)
            at = first % NBLK * 2 * half
            result = jnp.dot(
                embed[h, :, at : at + 2 * half * unit], both, preferred_element_type=f32
            )
            g = first // NBLK
            mixture[g] = result if mixture[g] is None else mixture[g] + result

    def summed(ref, sems, w):
        arrived = ref.at[pl.ds(w * size * pairs, size * pairs)]
        pltpu.make_async_copy(arrived, arrived, sems.at[w]).wait()
        whole = arrived[...].reshape(size, pairs, half, LANES).astype(f32)
        return jnp.sum(whole, 1).astype(bf16)

    def finished(w):
        @pl.when(here == 0)
        def _():
            gathered[w, 1] = summed(extra, recv2, w)

        @pl.when(here != 0)
        def _():
            gather(w).wait_recv()

        mixed(w, 1)

    for w in range(WAVES):
        gathered[w, 0] = summed(pieces, recv1, w)

        @pl.when(here != 0)
        def _():
            gather(w).start()

        mixed(w, 0)
        if w > 0:
            finished(w - 1)
    finished(WAVES - 1)
    for g in range(groups):
        out[:, LANES * g : LANES * (g + 1)] = (mixture[g] * scale[...]).astype(bf16)
    for p in range(2):
        share(p).wait_send()
    others = pieces.at[pl.ds(0, len(peers))]
    pltpu.make_async_copy(others, others, send1).wait()
    favour.wait_send()

    @pl.when(here != 0)
    def _():
        for w in range(WAVES):
            gather(w).wait_send()


def image_kernel(mixture, table, weight, out, image, save_sem):
    rows_here = mixture.shape[0]
    saves = []
    for c in range(2):
        for h in range(SAVES):
            part = slice(h * (rows_here // SAVES), (h + 1) * (rows_here // SAVES))
            result = jnp.dot(
                mixture[part], table[:, c * FAC : (c + 1) * FAC], preferred_element_type=jnp.float32
            )
            image[c, part] = result * weight[...]
            saves.append(
                pltpu.make_async_copy(
                    image.at[c, part], out.at[0, c, part], save_sem.at[c * SAVES + h]
                )
            )
            saves[-1].start()
    for save in saves:
        save.wait()


def shards(grid_count, vis_count, vis_coords, vis_values, tile_index):
    groups = grid_count // NBLK
    half = CONTRIB // 2
    rows_here = FAC // vis_count
    unitary = 1.0 / math.sqrt(SUB)
    bf16, f32 = jnp.bfloat16, jnp.float32
    far = pl.BlockSpec(memory_space=pltpu.HBM)
    inside = pl.BlockSpec(memory_space=pltpu.VMEM)
    dma = pltpu.SemaphoreType.DMA
    blocks = vis_coords.shape[1]
    visible = vis_coords.shape[3]
    tall = 2 * visible // LANES

    def tiled(array):
        array = array.reshape(blocks, 2, visible // LANES, LANES)
        return array.transpose(0, 2, 1, 3).reshape(blocks * tall, LANES)

    row_scale = taper() * (unitary / math.sqrt(CONTRIB * groups))
    row_scale = np.broadcast_to(row_scale[:, None], (FAC, LANES)).astype(np.float32)
    mixture = pl.pallas_call(
        functools.partial(subgrid_kernel, grid_count, vis_count, unitary),
        out_shape=jax.ShapeDtypeStruct((rows_here, groups * LANES), bf16),
        in_specs=[far] * 7,
        out_specs=inside,
        scratch_shapes=[
            pltpu.VMEM((1, blocks), jnp.int32),
            pltpu.VMEM((2, LANES), jnp.int32),
            pltpu.SMEM((2, LANES), jnp.int32),
            pltpu.VMEM((blocks * tall, LANES), f32),
            pltpu.VMEM((blocks * tall, LANES), f32),
            pltpu.VMEM((JOINT * tall, LANES), f32),
            pltpu.VMEM((5, JOINT * tall, LANES), f32),
            pltpu.VMEM((blocks + 1, TILE, 2 * TILE), f32),
            pltpu.VMEM((2 * SUB, 2 * LANES * groups), bf16),
            pltpu.VMEM((SUB, 2 * SUB), bf16),
            pltpu.VMEM((2, rows_here, SUB), bf16),
            pltpu.VMEM((rows_here, LANES), f32),
            pltpu.VMEM((SUB, 2 * SUB), bf16),
            pltpu.VMEM((grid_count, half, LANES), bf16),
            pltpu.VMEM((grid_count, half, LANES), bf16),
            pltpu.VMEM((grid_count, half, LANES), bf16),
            pltpu.VMEM((grid_count * vis_count // 2, half, LANES), bf16),
            pltpu.VMEM((grid_count * vis_count // 2, half, LANES), bf16),
            pltpu.VMEM((WAVES, 2, grid_count // WAVES, half, LANES), bf16),
            dma,
            dma,
            dma((blocks // JOINT, 2)),
            dma((5,)),
            dma((2, 2)),
            dma((WAVES, 2)),
            dma,
            dma,
            dma((WAVES,)),
            dma((WAVES,)),
        ],
        compiler_params=pltpu.CompilerParams(
            collective_id=0, has_side_effects=True, vmem_limit_bytes=ROOM
        ),
        cost_estimate=pl.CostEstimate(flops=10**10, bytes_accessed=10**6, transcendentals=10**6),
        name="subgrids",
    )(
        *[
            pltpu.with_memory_space_constraint(array, pltpu.HBM)
            for array in (
                tile_index,
                tiled(vis_coords),
                tiled(vis_values),
                jnp.asarray(column_table(groups)),
                jnp.asarray(row_table()),
                jnp.asarray(embed_table(min(NBLK, grid_count // WAVES))),
                jnp.asarray(row_scale),
            )
        ]
    )

    return pl.pallas_call(
        image_kernel,
        out_shape=jax.ShapeDtypeStruct((1, 2, rows_here, FAC), f32),
        in_specs=[inside] * 3,
        out_specs=far,
        scratch_shapes=[pltpu.VMEM((2, rows_here, FAC), f32), dma((2 * SAVES,))],
        compiler_params=pltpu.CompilerParams(vmem_limit_bytes=ROOM),
        name="images",
    )(
        mixture,
        jnp.asarray(output_table(groups)),
        jnp.asarray(taper()[None, :].astype(np.float32)),
    )


def solution(mesh):
    placed = (P("grid", "vis", None, None), P("grid", "vis", None, None), P("grid", "vis"))
    body = functools.partial(shards, mesh.shape["grid"], mesh.shape["vis"])
    return jax.shard_map(
        body, mesh=mesh, in_specs=placed, out_specs=P("grid", None, "vis", None), check_vma=False
    )
```
